256 devices in a mesh: sub: 32 (over x, z_hi, core), coarse: 8 (over z_lo, y).
Axes of the slice: x: 4, y: 4, z: 8 (z_hi: 4, z_lo: 2; z = z_hi * 2 + z_lo), core: 2. Of those that a mesh axis runs over, the one named last changes fastest.
Arguments:
- residual_parts: bfloat16 [32, 8, 4, 256, 512], P('sub', 'coarse'), may hold values from -6 to 6
- face_slot: int32 [32, 8, 4], P('sub', 'coarse'), may hold values from 0 to 3, each once within a row
- face_order: int32 [32, 8, 4, 512], P('sub', 'coarse'), may hold values from 0 to 511, each once within a row
- face_scale: float32 [32, 8, 4], P('sub', 'coarse'), may hold values from 0 to 1, as said below
- vertex_unknowns: int32 [32, 8, 256], P('sub', 'coarse'), may hold values from 0 to 2047, all different within a row
- front_inverse: bfloat16 [32, 8, 2048, 2048], P('sub', 'coarse')
- coarse_basis: bfloat16 [32, 8, 2048, 256], P('sub', 'coarse'), may hold values from -0.125 to 0.125
- coarse_inverse: bfloat16 [32, 2048, 2048], P('sub', None, 'coarse'), as said below
- thermal_handoff: bfloat16 [32, 2048, 128], P('sub'), may hold values from -0.125 to 0.125
- chain_transfer: float32 [32, 128, 128], P('sub')
- coupling_in: bfloat16 [32, 128, 2048], P('sub', None, 'coarse'), may hold values from -0.5 to 0.5
Outputs:
- correction: bfloat16 [32, 8, 4, 256, 512], P('sub', 'coarse')
The draws below stay inside these ranges and needn't reach their ends.
Inputs may be any that keep to these rules, and one draw needn't show every extreme that they name: `face_slot`: each row is a permutation of 0 to 3. `face_order`: each row is a permutation of 0 to 511. `vertex_unknowns`: the 256 entries of each subdomain are distinct. `face_scale`: the two weights of a shared face sum to one; a face on the outer boundary has weight one. `coarse_inverse`: each line's matrix is symmetric.
All inputs are finite; a program needn't handle non-finite values.
Results may differ from the reference program's by a relative error of at most 0.0059.
Values may be sent and summed in bfloat16 or wider, within the bound.
No kernel may reach another device: no remote copies, remote signals or barrier semaphores. Data moves between devices by JAX's collectives and lax.ppermute only.
A program may use at most 128 MiB of HBM per device.

```python
import math
import jax
import jax.numpy as jnp
from jax import lax

FACE_DOFS = 512
VERTEX_COUNT = 256
CHANNELS = 128
SAMPLES = 256
N_SUB = 32
N_COARSE = 8


def draw_face_scale(key, part):
    top_level = math.log(100.0)
    stiffness = jnp.exp(jax.random.uniform(jax.random.fold_in(key, 11), (N_SUB, N_COARSE), jnp.float32, 0.0, top_level))
    lower = jnp.concatenate([stiffness[:1], stiffness[:-1]], 0)
    upper = jnp.concatenate([stiffness[1:], stiffness[-1:]], 0)
    left_side = jnp.concatenate([stiffness[:, :1], stiffness[:, :-1]], 1)
    right_side = jnp.concatenate([stiffness[:, 1:], stiffness[:, -1:]], 1)
    row_index = lax.broadcasted_iota(jnp.int32, (N_SUB, N_COARSE), 0)
    col_index = lax.broadcasted_iota(jnp.int32, (N_SUB, N_COARSE), 1)
    weights = [jnp.where(row_index > 0, stiffness / (stiffness + lower), 1.0), jnp.where(row_index < N_SUB - 1, stiffness / (stiffness + upper), 1.0), jnp.where(col_index > 0, stiffness / (stiffness + left_side), 1.0), jnp.where(col_index < N_COARSE - 1, stiffness / (stiffness + right_side), 1.0)]
    return jnp.stack(weights, 2).astype(jnp.float32)


def draw_front_inverse(key, part):
    interface = 4 * FACE_DOFS
    shape_all = (N_SUB, N_COARSE, interface, interface)
    noise = jax.random.normal(jax.random.fold_in(key, 31), shape_all, jnp.float32)
    diagonal = (lax.broadcasted_iota(jnp.int32, (interface, interface), 0) == lax.broadcasted_iota(jnp.int32, (interface, interface), 1)).astype(jnp.float32)
    return (noise * (0.6 / math.sqrt(interface)) + diagonal).astype(jnp.bfloat16)


def draw_coarse_inverse(key, part):
    line_order = N_COARSE * VERTEX_COUNT
    shape_all = (N_SUB, line_order, line_order)
    noise = jax.random.normal(jax.random.fold_in(key, 41), shape_all, jnp.float32)
    symmetric = (noise + jnp.swapaxes(noise, 1, 2)) * (0.35 / math.sqrt(line_order))
    diagonal = (lax.broadcasted_iota(jnp.int32, (line_order, line_order), 0) == lax.broadcasted_iota(jnp.int32, (line_order, line_order), 1)).astype(jnp.float32)
    return (symmetric + diagonal).astype(jnp.bfloat16)


def draw_chain_transfer(key, part):
    share_slow = 0.5
    slow_mask = jax.random.bernoulli(jax.random.fold_in(key, 21), share_slow, (CHANNELS,))
    slow_rate = jnp.exp(-jax.random.uniform(jax.random.fold_in(key, 22), (N_SUB, CHANNELS), jnp.float32, 0.2, 1.5) / N_SUB)
    fast_rate = jnp.exp(-jax.random.uniform(jax.random.fold_in(key, 23), (N_SUB, CHANNELS), jnp.float32, 1.0, 3.0))
    cooling_speeds = jnp.where(slow_mask[None, :], slow_rate, fast_rate)
    cooling_pulses = jax.random.bernoulli(jax.random.fold_in(key, 24), 3.0 / N_SUB, (N_SUB, 1))
    cooling_speeds = cooling_speeds * jnp.where(cooling_pulses, 0.6, 1.0)
    mixing = jax.random.normal(jax.random.fold_in(key, 25), (N_SUB, CHANNELS, CHANNELS), jnp.float32) * (0.2 / math.sqrt(CHANNELS))
    diagonal = (lax.broadcasted_iota(jnp.int32, (CHANNELS, CHANNELS), 0) == lax.broadcasted_iota(jnp.int32, (CHANNELS, CHANNELS), 1)).astype(jnp.float32)
    return mixing + diagonal[None] * cooling_speeds[:, :, None]


def levels(stream_key, shape, shards, low, high):
    level, own = 1.0, jax.random.fold_in(stream_key, 6)
    for axis_at, parts in shards:
        steps = jnp.exp(jax.random.uniform(jax.random.fold_in(own, axis_at), (parts,), jnp.float32, low / len(shards), high / len(shards)))
        level = level * jnp.repeat(steps, shape[axis_at] // parts).reshape([-1 if axis == axis_at else 1 for axis in range(len(shape))])
    return level


def choose_distinct(key, rows, number_of, top, lift):
    sequence = jax.random.permutation(jax.random.fold_in(key, 1), number_of)
    pull = sequence
    for power in range(3):
        pull = pull * pull // number_of
    pull = pull * lift // number_of
    chance = jax.random.randint(jax.random.fold_in(key, 2), (rows, number_of), 0, 4096) + pull
    sure = jax.random.permutation(jax.random.fold_in(key, 3), rows)[jnp.arange(number_of) % rows]
    chance = jnp.where(jnp.arange(rows)[:, None] == sure[None, :], 1 << 14, chance)
    score = chance * number_of + jnp.arange(number_of)
    return lax.top_k(score.astype(jnp.int32), top)[1].astype(jnp.int32)


def scatter_about(own_key, shape, scale, reach, cuts=(), dtype=jnp.bfloat16):
    array = scale * jax.random.normal(own_key, shape, jnp.float32)
    if cuts:
        array = array * levels(own_key, shape, cuts, -0.22, 0.18)
    return jnp.clip(array, -reach, reach).astype(dtype)


def setup_inputs(seed: int = 0) -> dict:
    arg_keys = jax.random.split(jax.random.key(seed), 12)
    residual_parts = scatter_about(arg_keys[0], (N_SUB, N_COARSE, 4, SAMPLES, FACE_DOFS), 1.0, 6.0, ((0, 32), (1, 8)))
    face_slot = jax.vmap(lambda own: jax.random.permutation(own, 4))(jax.random.split(arg_keys[1], N_SUB * N_COARSE)).reshape((N_SUB, N_COARSE, 4)).astype(jnp.int32)
    face_order = jax.vmap(lambda own: jax.random.permutation(own, FACE_DOFS))(jax.random.split(arg_keys[2], N_SUB * N_COARSE * 4)).reshape((N_SUB, N_COARSE, 4, FACE_DOFS)).astype(jnp.int32)
    face_scale = draw_face_scale(jax.random.fold_in(arg_keys[11], 71), 0)
    vertex_unknowns = choose_distinct(arg_keys[4], N_SUB * N_COARSE, 4 * FACE_DOFS, VERTEX_COUNT, 0).reshape((N_SUB, N_COARSE, VERTEX_COUNT))
    front_inverse = draw_front_inverse(jax.random.fold_in(arg_keys[11], 71), 0)
    coarse_basis = scatter_about(arg_keys[6], (N_SUB, N_COARSE, 4 * FACE_DOFS, VERTEX_COUNT), (4 * FACE_DOFS) ** -0.5, 0.125, ((0, 32), (1, 8)))
    coarse_inverse = draw_coarse_inverse(jax.random.fold_in(arg_keys[11], 71), 0)
    thermal_handoff = scatter_about(arg_keys[8], (N_SUB, N_COARSE * VERTEX_COUNT, CHANNELS), (N_COARSE * VERTEX_COUNT) ** -0.5, 0.125, ((0, 32),))
    chain_transfer = draw_chain_transfer(jax.random.fold_in(arg_keys[11], 71), 0)
    coupling_in = scatter_about(arg_keys[10], (N_SUB, CHANNELS, N_COARSE * VERTEX_COUNT), CHANNELS ** -0.5, 0.5, ((0, 32), (2, 8)))
    return dict(residual_parts=residual_parts, face_slot=face_slot, face_order=face_order, face_scale=face_scale, vertex_unknowns=vertex_unknowns, front_inverse=front_inverse, coarse_basis=coarse_basis, coarse_inverse=coarse_inverse, thermal_handoff=thermal_handoff, chain_transfer=chain_transfer, coupling_in=coupling_in)


HIGHEST = lax.Precision.HIGHEST


def canonical(values, face_slot, face_order):
    ordered = jnp.take_along_axis(values, face_order[:, :, :, None, :], axis=4)
    return jnp.take_along_axis(ordered, face_slot[:, :, :, None, None], axis=2)


def restore_layout(values, face_slot, face_order):
    slot_back = jnp.argsort(face_slot, axis=2)
    order_back = jnp.argsort(face_order, axis=3)
    by_face = jnp.take_along_axis(values, slot_back[:, :, :, None, None], axis=2)
    return jnp.take_along_axis(by_face, order_back[:, :, :, None, :], axis=4)


def neighbours(values):
    zero_sub = jnp.zeros_like(values[:1, :, 0])
    from_lower = jnp.concatenate([zero_sub, values[:-1, :, 1]], 0)
    from_upper = jnp.concatenate([values[1:, :, 0], zero_sub], 0)
    zero_across = jnp.zeros_like(values[:, :1, 2])
    from_left = jnp.concatenate([zero_across, values[:, :-1, 3]], 1)
    from_right = jnp.concatenate([values[:, 1:, 2], zero_across], 1)
    return jnp.stack([from_lower, from_upper, from_left, from_right], 2)


def reference(residual_parts, face_slot, face_order, face_scale, vertex_unknowns, front_inverse, coarse_basis, coarse_inverse, thermal_handoff, chain_transfer, coupling_in):
    scale_grid = face_scale[:, :, :, None, None]
    canon = canonical(residual_parts, face_slot, face_order)
    averaged = (scale_grid * (canon.astype(jnp.float32) + neighbours(canon).astype(jnp.float32))).astype(jnp.bfloat16)
    local_residual = restore_layout(averaged, face_slot, face_order)
    sub_rows, sub_cols, face_count, sample_count, block_size = residual_parts.shape
    subdomains = sub_rows * sub_cols
    flat_residual = local_residual.reshape(subdomains, face_count, sample_count, block_size)
    flat_inverse = front_inverse.reshape(subdomains, face_count, block_size, face_count, block_size)
    flat_basis = coarse_basis.reshape(subdomains, face_count, block_size, -1)
    vertex_vector = vertex_unknowns.reshape(subdomains, -1)

    def local_work(items):
        residual, inverse, basis, primal_values = items
        positions = lax.broadcasted_iota(jnp.int32, (primal_values.shape[0], face_count * block_size), 1)
        hits = jnp.sum((primal_values[:, None] == positions).astype(jnp.int32), axis=0)
        dual_mask = (1 - hits).astype(jnp.bfloat16).reshape(face_count, 1, block_size)
        masked = (residual * dual_mask).astype(jnp.float32)
        dual = jnp.einsum("gnj,gjfk->fnk", masked, inverse.astype(jnp.float32), precision=HIGHEST) * dual_mask.astype(jnp.float32)
        wide_space = jnp.einsum("gnj,gjc->nc", residual.astype(jnp.float32), basis.astype(jnp.float32), precision=HIGHEST).astype(jnp.bfloat16)
        return dual, wide_space

    dual_part, coarse_residual = lax.map(local_work, (flat_residual, flat_inverse, flat_basis, vertex_vector))
    primal_count = coarse_residual.shape[-1]
    residual_of_line = coarse_residual.reshape(sub_rows, sub_cols, sample_count, primal_count).transpose(0, 2, 1, 3).reshape(sub_rows, sample_count, sub_cols * primal_count)
    line_base = jnp.einsum("pnl,plm->pnm", residual_of_line.astype(jnp.float32), coarse_inverse.astype(jnp.float32), precision=HIGHEST)
    inflow = jnp.einsum("pnl,plk->pnk", residual_of_line.astype(jnp.float32), thermal_handoff.astype(jnp.float32), precision=HIGHEST)

    def carry_step(state_now, items):
        transfer, incoming = items
        return jnp.dot(state_now, transfer, precision=HIGHEST) + incoming, state_now

    final_state, carried = lax.scan(carry_step, jnp.zeros_like(inflow[0]), (chain_transfer, inflow))
    line_solution = (line_base + jnp.einsum("pnk,pkm->pnm", carried, coupling_in.astype(jnp.float32), precision=HIGHEST)).astype(jnp.bfloat16)
    own_coarse = line_solution.reshape(sub_rows, sample_count, sub_cols, primal_count).transpose(0, 2, 1, 3).reshape(subdomains, sample_count, primal_count)

    def extend_to_faces(items):
        wide_space, basis = items
        return jnp.einsum("nc,gjc->gnj", wide_space.astype(jnp.float32), basis.astype(jnp.float32), precision=HIGHEST)

    coarse_part = lax.map(extend_to_faces, (own_coarse, flat_basis))
    subregion_iterate = (dual_part + coarse_part).reshape(sub_rows, sub_cols, face_count, sample_count, block_size)
    weighted = (scale_grid * canonical(subregion_iterate, face_slot, face_order)).astype(jnp.bfloat16)
    summed = (weighted.astype(jnp.float32) + neighbours(weighted).astype(jnp.float32)).astype(jnp.bfloat16)
    return restore_layout(summed, face_slot, face_order)
```

```python
import jax
import jax.numpy as jnp
from jax import lax
from jax.experimental import pallas as pl
from jax.experimental.pallas import tpu as pltpu
from jax.sharding import PartitionSpec as P

BF16 = jnp.bfloat16
F32 = jnp.float32


def params(megabytes):
    return pltpu.CompilerParams(vmem_limit_bytes=megabytes << 20)


def cost(flops, bytes_accessed):
    return pl.CostEstimate(flops=flops, bytes_accessed=bytes_accessed, transcendentals=0)


def resident(shape):
    return pl.BlockSpec(shape, lambda *_: (0,) * len(shape))


IN_VMEM = pl.BlockSpec(memory_space=pltpu.VMEM)


def in_hbm(value):
    return pltpu.with_memory_space_constraint(value, pltpu.HBM)


def times(a, b):
    return jnp.dot(a, b, preferred_element_type=F32)


def times_columns(a, b):
    return lax.dot_general(a, b, (((0,), (0,)), ((), ())), preferred_element_type=F32)


def split(value):
    high = value.astype(BF16)
    return high, (value - high.astype(F32)).astype(BF16)


def sorting_table(order, face):
    size = order.shape[1]
    local = lax.broadcasted_iota(jnp.int32, (size, size), 0)
    return jnp.where(local == order[pl.ds(face, 1), :], 1.0, 0.0)


def canon_kernel(slot, parts, order, *outs):
    d = pl.program_id(0)
    table = sorting_table(order, slot[d]).astype(BF16)
    value = times(parts[0], table).astype(BF16)
    for i, out in enumerate(outs):

        @pl.when(d == i)
        def _():
            out[...] = value


def to_canonical(slot, parts, order):
    faces, samples, size = parts.shape
    return pl.pallas_call(
        canon_kernel,
        out_shape=[jax.ShapeDtypeStruct((samples, size), BF16)] * faces,
        grid_spec=pltpu.PrefetchScalarGridSpec(
            num_scalar_prefetch=1,
            grid=(faces,),
            in_specs=[
                pl.BlockSpec((1, samples, size), lambda d, slot: (slot[d], 0, 0)),
                resident((faces, size)),
            ],
            out_specs=[IN_VMEM] * faces,
        ),
        compiler_params=params(8),
        cost_estimate=cost(2 * faces * samples * size * size, 4 * faces * samples * size),
        name="canon",
    )(slot, in_hbm(parts), in_hbm(order))


def tables_kernel(slot, order, basis, sort, restore, ordered, ordered_columns):
    d = pl.program_id(0)
    table = sorting_table(order, slot[d])
    sort[0] = table.astype(BF16)
    restore[0] = table.T.astype(BF16)
    ordered[0] = times(restore[0], basis[0]).astype(BF16)
    ordered_columns[0] = times_columns(basis[0], sort[0]).astype(BF16)


def tables(slot, order, basis):
    faces, size, primal = basis.shape

    def by_direction(*shape):
        return pl.BlockSpec((1,) + shape, lambda d, slot: (d, 0, 0))

    return pl.pallas_call(
        tables_kernel,
        out_shape=[
            pltpu.HBM((faces, size, size), BF16),
            pltpu.HBM((faces, size, size), BF16),
            jax.ShapeDtypeStruct((faces, size, primal), BF16),
            pltpu.HBM((faces, primal, size), BF16),
        ],
        grid_spec=pltpu.PrefetchScalarGridSpec(
            num_scalar_prefetch=1,
            grid=(faces,),
            in_specs=[
                resident((faces, size)),
                pl.BlockSpec((1, size, primal), lambda d, slot: (slot[d], 0, 0)),
            ],
            out_specs=[
                by_direction(size, size),
                by_direction(size, size),
                by_direction(size, primal),
                by_direction(primal, size),
            ],
        ),
        compiler_params=params(12),
        cost_estimate=cost(
            4 * faces * size * size * primal, 4 * faces * size * size + 6 * faces * size * primal
        ),
        name="tables",
    )(slot, in_hbm(order), in_hbm(basis))


def has_neighbour(d):
    axis = "sub" if d < 2 else "coarse"
    place = lax.axis_index(axis)
    return place > 0 if d % 2 == 0 else place < lax.axis_size(axis) - 1


def sum_across(own, beside, d):
    own, beside = own[...].astype(F32), beside[...].astype(F32)
    return own + jnp.where(has_neighbour(d), beside, 0.0)


def residual_kernel(scale, *refs):
    d = pl.program_id(0)
    faces = scale.shape[0]
    canon, beside = refs[:faces], refs[faces : 2 * faces]
    ordered, handoff, averaged, coarse, heat, total = refs[2 * faces :]
    for i in range(faces):

        @pl.when(d == i)
        def _():
            value = (scale[i] * sum_across(canon[i], beside[i], i)).astype(BF16)
            averaged[0] = value
            term = times(value, ordered[i])
            total[...] = term if i == 0 else total[...] + term

    @pl.when(d == faces - 1)
    def _():
        rounded = total[...].astype(BF16)
        coarse[...] = rounded
        primal = rounded.shape[1]
        start = pl.multiple_of(lax.axis_index("coarse") * primal, primal)
        heat[...] = times(rounded, handoff[pl.ds(start, primal), :])


def residuals(scale, canon, beside, ordered, handoff):
    faces, size, primal = ordered.shape
    samples = canon[0].shape[0]
    channels = handoff.shape[1]
    return pl.pallas_call(
        residual_kernel,
        out_shape=[
            pltpu.HBM((faces, samples, size), BF16),
            jax.ShapeDtypeStruct((samples, primal), BF16),
            jax.ShapeDtypeStruct((samples, channels), F32),
        ],
        grid=(faces,),
        in_specs=[pl.BlockSpec(memory_space=pltpu.SMEM)] + [IN_VMEM] * (2 * faces + 2),
        out_specs=[pl.BlockSpec((1, samples, size), lambda d: (d, 0, 0)), IN_VMEM, IN_VMEM],
        scratch_shapes=[pltpu.VMEM((samples, primal), F32)],
        compiler_params=params(8),
        cost_estimate=cost(
            2 * faces * samples * size * primal, 6 * faces * samples * size + 2 * faces * size * primal
        ),
        name="residuals",
    )(scale, *canon, *beside, ordered, handoff)


def share_kernel(inflow, out):
    total = inflow[0]
    for q in range(1, inflow.shape[0]):
        total = total + inflow[q]
    out[...] = jnp.broadcast_to(total[None], out.shape)


def shared_sum(inflow, lines):
    members, share, channels = inflow.shape
    return pl.pallas_call(
        share_kernel,
        out_shape=jax.ShapeDtypeStruct((lines, share, channels), F32),
        compiler_params=params(8),
        cost_estimate=cost(members * share * channels, 4 * (lines + members) * share * channels),
        name="shared_sum",
    )(inflow)


def dual_kernel(slot, scale, averaged, restore, sort, mask, inverse, out, masked):
    i = pl.program_id(0)
    faces, _, size = masked.shape

    @pl.when(i < faces)
    def _():
        local = times(averaged[0], restore[0])
        masked[slot[i]] = (local * mask[slot[i]]).astype(BF16)

    @pl.when(i >= faces)
    def _():
        d = i - faces
        total = None
        for g in range(faces):
            term = times(masked[g], inverse[g * size : (g + 1) * size, :])
            total = term if total is None else total + term
        high, low = split(total * (mask[slot[d]] * scale[d]))
        out[0] = times(high, sort[0]) + times(low, sort[0])


def dual(slot, scale, averaged, sort, restore, mask, inverse):
    faces, samples, size = averaged.shape

    def first(i):
        return jnp.minimum(i, faces - 1)

    def second(i):
        return jnp.maximum(i - faces, 0)

    return pl.pallas_call(
        dual_kernel,
        out_shape=pltpu.HBM(averaged.shape, F32),
        grid_spec=pltpu.PrefetchScalarGridSpec(
            num_scalar_prefetch=1,
            grid=(2 * faces,),
            in_specs=[
                pl.BlockSpec(memory_space=pltpu.SMEM),
                pl.BlockSpec((1, samples, size), lambda i, slot: (first(i), 0, 0)),
                pl.BlockSpec((1, size, size), lambda i, slot: (first(i), 0, 0)),
                pl.BlockSpec((1, size, size), lambda i, slot: (second(i), 0, 0)),
                resident(mask.shape),
                pl.BlockSpec((faces * size, size), lambda i, slot: (0, slot[second(i)])),
            ],
            out_specs=pl.BlockSpec((1, samples, size), lambda i, slot: (second(i), 0, 0)),
            scratch_shapes=[pltpu.VMEM((faces, samples, size), BF16)],
        ),
        compiler_params=params(16),
        cost_estimate=cost(
            2 * samples * faces * size * (faces + 3) * size,
            2 * faces * size * (faces + 2) * size + 6 * faces * samples * size,
        ),
        name="dual",
    )(slot, scale, in_hbm(averaged), in_hbm(restore), in_hbm(sort), mask, in_hbm(inverse))


def chain_kernel(inflow, transfer, out, state):
    i = pl.program_id(0)
    lines = inflow.shape[0]

    @pl.when(i == 0)
    def _():
        state[...] = jnp.zeros_like(state)

    def step(k, value):
        high, low = split(value)
        map_high, map_low = split(transfer[k])
        value = times(high, map_high) + (times(low, map_high) + times(high, map_low))
        return value + inflow[k]

    ahead = jnp.clip(lax.axis_index("sub") - i * lines, 0, lines)
    state[...] = lax.fori_loop(0, ahead, step, state[...])

    @pl.when(i == pl.num_programs(0) - 1)
    def _():
        out[...] = jnp.broadcast_to(state[...][None], out.shape)


def chain(inflow, transfer, members):
    lines, samples, channels = inflow.shape
    steps = 4
    return pl.pallas_call(
        chain_kernel,
        out_shape=jax.ShapeDtypeStruct((members, samples, channels), F32),
        grid=(steps,),
        in_specs=[
            pl.BlockSpec((lines // steps, samples, channels), lambda i: (i, 0, 0)),
            pl.BlockSpec((lines // steps, channels, channels), lambda i: (i, 0, 0)),
        ],
        out_specs=IN_VMEM,
        scratch_shapes=[pltpu.VMEM((samples, channels), F32)],
        compiler_params=params(8),
        cost_estimate=cost(
            6 * lines * samples * channels * channels, 4 * lines * channels * (samples + channels)
        ),
        name="chain",
    )(inflow, in_hbm(transfer))


def line_kernel(gathered, inverse, out):
    members, _, primal = gathered.shape
    member = lax.axis_index("coarse")
    total = None
    for i, bits in enumerate(GATHER_BITS):
        start = pl.multiple_of(jnp.bitwise_xor(member, bits) * primal, primal)
        term = times(gathered[i], inverse[pl.ds(start, primal), :])
        total = term if total is None else total + term
    out[...] = total


def line_base(gathered, inverse):
    members, samples, primal = gathered.shape
    return pl.pallas_call(
        line_kernel,
        out_shape=jax.ShapeDtypeStruct((samples, primal), F32),
        grid=(1,),
        in_specs=[resident(gathered.shape), resident(inverse.shape)],
        out_specs=IN_VMEM,
        compiler_params=params(12),
        cost_estimate=cost(
            2 * members * samples * primal * primal, 2 * members * primal * (samples + primal)
        ),
        name="line_base",
    )(gathered, in_hbm(inverse))


def extend_kernel(scale, base, carried, coupling, ordered_columns, dual_part, *rest):
    outs, answer = rest[:-1], rest[-1]
    d = pl.program_id(0)

    @pl.when(d == 0)
    def _():
        high, low = split(carried[...])
        term = times(high, coupling[...]) + times(low, coupling[...])
        answer[...] = (base[...] + term).astype(BF16)

    value = dual_part[0] + scale[d] * times(answer[...], ordered_columns[0])
    value = value.astype(BF16)
    for i, out in enumerate(outs):

        @pl.when(d == i)
        def _():
            out[...] = value


def extend(scale, base, carried, coupling, ordered_columns, dual_part):
    faces, samples, size = dual_part.shape
    primal = base.shape[1]
    channels = carried.shape[1]
    return pl.pallas_call(
        extend_kernel,
        out_shape=[jax.ShapeDtypeStruct((samples, size), BF16)] * faces,
        grid=(faces,),
        in_specs=[
            pl.BlockSpec(memory_space=pltpu.SMEM),
            IN_VMEM,
            IN_VMEM,
            resident((channels, primal)),
            pl.BlockSpec((1, primal, size), lambda d: (d, 0, 0)),
            pl.BlockSpec((1, samples, size), lambda d: (d, 0, 0)),
        ],
        out_specs=[IN_VMEM] * faces,
        scratch_shapes=[pltpu.VMEM((samples, primal), BF16)],
        compiler_params=params(8),
        cost_estimate=cost(
            2 * faces * samples * size * primal, 6 * faces * samples * size + 2 * faces * size * primal
        ),
        name="extend",
    )(scale, base, carried, in_hbm(coupling), in_hbm(ordered_columns), in_hbm(dual_part))


def finish_kernel(slot, *refs):
    d = pl.program_id(0)
    restore, out = refs[-2:]
    faces = (len(refs) - 2) // 2
    for i in range(faces):

        @pl.when(d == i)
        def _():
            value = sum_across(refs[i], refs[faces + i], i).astype(BF16)
            out[0] = times(value, restore[i]).astype(BF16)


def finish(slot, weighted, beside, restore):
    faces, size, _ = restore.shape
    samples = weighted[0].shape[0]
    return pl.pallas_call(
        finish_kernel,
        out_shape=jax.ShapeDtypeStruct((faces, samples, size), BF16),
        grid_spec=pltpu.PrefetchScalarGridSpec(
            num_scalar_prefetch=1,
            grid=(faces,),
            in_specs=[IN_VMEM] * (2 * faces + 1),
            out_specs=pl.BlockSpec((1, samples, size), lambda d, s: (s[d], 0, 0)),
        ),
        compiler_params=params(8),
        cost_estimate=cost(
            2 * faces * samples * size * size, 6 * faces * samples * size + 2 * faces * size * size
        ),
        name="finish",
    )(slot, *weighted, *beside, restore)


GATHER_STAGES = (2, 1, 4)
GATHER_BITS = (0, 2, 1, 3, 4, 6, 5, 7)


def gather_stage(value, bit):
    pairs = [(i, i ^ bit) for i in range(lax.axis_size("coarse"))]
    return lax.ppermute(value, "coarse", pairs)


def neighbours(faces):
    lower, upper, left, right = faces

    def shifted(value, axis, step):
        count = lax.axis_size(axis)
        pairs = [(i, (i + step) % count) for i in range(count)]
        return lax.ppermute(value, axis, pairs)

    return (
        shifted(upper, "sub", 1),
        shifted(lower, "sub", -1),
        shifted(right, "coarse", 1),
        shifted(left, "coarse", -1),
    )


def per_device(
    residual_parts,
    face_slot,
    face_order,
    face_scale,
    vertex_unknowns,
    front_inverse,
    coarse_basis,
    coarse_inverse,
    thermal_handoff,
    chain_transfer,
    coupling_in,
):
    parts = residual_parts[0, 0]
    slot = face_slot[0, 0]
    order = face_order[0, 0]
    scale = face_scale[0, 0]
    faces, samples, size = parts.shape
    basis = coarse_basis[0, 0].reshape(faces, size, -1)
    lines, members = lax.axis_size("sub"), lax.axis_size("coarse")
    share = samples // members

    transfers = lax.all_gather(chain_transfer[0], "sub")

    canon = to_canonical(slot, parts, order)
    beside = neighbours(canon)
    basis, canon = lax.optimization_barrier((basis, canon))
    sort, restore, ordered, ordered_columns = tables(slot, order, basis)
    averaged, coarse_residual, heat = residuals(
        scale, canon, beside, ordered, thermal_handoff[0]
    )

    channels = heat.shape[1]
    gathered = coarse_residual[None]
    received = gather_stage(gathered, GATHER_STAGES[0])
    inflow = lax.all_to_all(heat.reshape(members, share, channels), "coarse", 0, 0)
    inflow = shared_sum(inflow, lines)
    averaged, received, inflow = lax.optimization_barrier((averaged, received, inflow))
    inflow = lax.all_to_all(inflow, "sub", 0, 0)
    gathered = jnp.concatenate([gathered, received])
    received = gather_stage(gathered, GATHER_STAGES[1])

    positions = lax.broadcasted_iota(jnp.int32, (vertex_unknowns.shape[2], faces * size), 1)
    hits = jnp.sum((vertex_unknowns[0, 0][:, None] == positions).astype(F32), axis=0)
    mask = (1.0 - hits).reshape(faces, 1, size)
    dual_part = dual(slot, scale, averaged, sort, restore, mask, front_inverse[0, 0])

    inflow, received, dual_part = lax.optimization_barrier((inflow, received, dual_part))
    gathered = jnp.concatenate([gathered, received])
    gathered = jnp.concatenate([gathered, gather_stage(gathered, GATHER_STAGES[2])])
    carried = chain(inflow, transfers, members)
    carried = lax.all_to_all(carried, "coarse", 0, 0).reshape(samples, channels)
    base = line_base(gathered, coarse_inverse[0])

    weighted = extend(scale, base, carried, coupling_in[0], ordered_columns, dual_part)
    beside = neighbours(weighted)
    return finish(slot, weighted, beside, restore)[None, None]


def solution(mesh):
    placed = (
        P("sub", "coarse", None, None, None),
        P("sub", "coarse", None),
        P("sub", "coarse", None, None),
        P("sub", "coarse", None),
        P("sub", "coarse", None),
        P("sub", "coarse", None, None),
        P("sub", "coarse", None, None),
        P("sub", None, "coarse"),
        P("sub", None, None),
        P("sub", None, None),
        P("sub", None, "coarse"),
    )
    return jax.shard_map(
        per_device,
        mesh=mesh,
        in_specs=placed,
        out_specs=P("sub", "coarse", None, None, None),
        check_vma=False,
    )
```

```python
import functools

import jax
import jax.numpy as jnp
from jax import lax
from jax.experimental import pallas as pl
from jax.experimental.pallas import tpu as pltpu
from jax.sharding import PartitionSpec as P

BF16 = jnp.bfloat16
F32 = jnp.float32


def params(megabytes):
    return pltpu.CompilerParams(vmem_limit_bytes=megabytes << 20)


def cost(flops, bytes_accessed):
    return pl.CostEstimate(flops=flops, bytes_accessed=bytes_accessed, transcendentals=0)


def resident(shape):
    return pl.BlockSpec(shape, lambda *_: (0,) * len(shape))


IN_VMEM = pl.BlockSpec(memory_space=pltpu.VMEM)


def in_hbm(value):
    return pltpu.with_memory_space_constraint(value, pltpu.HBM)


def times(a, b):
    return jnp.dot(a, b, preferred_element_type=F32)


def times_columns(a, b):
    return lax.dot_general(a, b, (((0,), (0,)), ((), ())), preferred_element_type=F32)


def split(value):
    high = value.astype(BF16)
    return high, (value - high.astype(F32)).astype(BF16)


def sorting_table(order, face):
    size = order.shape[1]
    local = lax.broadcasted_iota(jnp.int32, (size, size), 0)
    return jnp.where(local == order[pl.ds(face, 1), :], 1.0, 0.0)


def canon_kernel(slot, parts, order, *outs):
    d = pl.program_id(0)
    table = sorting_table(order, slot[d]).astype(BF16)
    value = times(parts[0], table).astype(BF16)
    for i, out in enumerate(outs):

        @pl.when(d == i)
        def _():
            out[...] = value


def to_canonical(slot, parts, order):
    faces, samples, size = parts.shape
    return pl.pallas_call(
        canon_kernel,
        out_shape=[jax.ShapeDtypeStruct((samples, size), BF16)] * faces,
        grid_spec=pltpu.PrefetchScalarGridSpec(
            num_scalar_prefetch=1,
            grid=(faces,),
            in_specs=[
                pl.BlockSpec((1, samples, size), lambda d, slot: (slot[d], 0, 0)),
                resident((faces, size)),
            ],
            out_specs=[IN_VMEM] * faces,
        ),
        compiler_params=params(8),
        cost_estimate=cost(2 * faces * samples * size * size, 4 * faces * samples * size),
        name="canon",
    )(slot, in_hbm(parts), in_hbm(order))


def tables_kernel(slot, order, basis, sort, restore, ordered, ordered_columns):
    d = pl.program_id(0)
    table = sorting_table(order, slot[d])
    sort[0] = table.astype(BF16)
    restore[0] = table.T.astype(BF16)
    ordered[0] = times(restore[0], basis[0]).astype(BF16)
    ordered_columns[0] = times_columns(basis[0], sort[0]).astype(BF16)


def tables(slot, order, basis):
    faces, size, primal = basis.shape

    def by_direction(*shape):
        return pl.BlockSpec((1,) + shape, lambda d, slot: (d, 0, 0))

    return pl.pallas_call(
        tables_kernel,
        out_shape=[
            pltpu.HBM((faces, size, size), BF16),
            pltpu.HBM((faces, size, size), BF16),
            jax.ShapeDtypeStruct((faces, size, primal), BF16),
            pltpu.HBM((faces, primal, size), BF16),
        ],
        grid_spec=pltpu.PrefetchScalarGridSpec(
            num_scalar_prefetch=1,
            grid=(faces,),
            in_specs=[
                resident((faces, size)),
                pl.BlockSpec((1, size, primal), lambda d, slot: (slot[d], 0, 0)),
            ],
            out_specs=[
                by_direction(size, size),
                by_direction(size, size),
                by_direction(size, primal),
                by_direction(primal, size),
            ],
        ),
        compiler_params=params(12),
        cost_estimate=cost(
            4 * faces * size * size * primal, 4 * faces * size * size + 6 * faces * size * primal
        ),
        name="tables",
    )(slot, in_hbm(order), in_hbm(basis))


def has_neighbour(d):
    axis = "sub" if d < 2 else "coarse"
    place = lax.axis_index(axis)
    return place > 0 if d % 2 == 0 else place < lax.axis_size(axis) - 1


def sum_across(own, beside, d):
    own, beside = own[...].astype(F32), beside[...].astype(F32)
    return own + jnp.where(has_neighbour(d), beside, 0.0)


def residual_kernel(scale, *refs):
    faces = scale.shape[0]
    canon, beside = refs[:faces], refs[faces : 2 * faces]
    ordered, handoff, averaged, coarse, heat = refs[2 * faces :]
    total = None
    for d in range(faces):
        value = (scale[d] * sum_across(canon[d], beside[d], d)).astype(BF16)
        averaged[d] = value
        term = times(value, ordered[d])
        total = term if total is None else total + term
    rounded = total.astype(BF16)
    coarse[...] = rounded
    primal = rounded.shape[1]
    start = pl.multiple_of(lax.axis_index("coarse") * primal, primal)
    heat[...] = times(rounded, handoff[pl.ds(start, primal), :])


def residuals(scale, canon, beside, ordered, handoff):
    faces, size, primal = ordered.shape
    samples = canon[0].shape[0]
    channels = handoff.shape[1]
    return pl.pallas_call(
        residual_kernel,
        out_shape=[
            pltpu.HBM((faces, samples, size), BF16),
            jax.ShapeDtypeStruct((samples, primal), BF16),
            jax.ShapeDtypeStruct((samples, channels), F32),
        ],
        grid=(1,),
        in_specs=[pl.BlockSpec(memory_space=pltpu.SMEM)] + [IN_VMEM] * (2 * faces + 2),
        out_specs=[resident((faces, samples, size)), IN_VMEM, IN_VMEM],
        compiler_params=params(8),
        cost_estimate=cost(
            2 * faces * samples * size * primal, 6 * faces * samples * size + 2 * faces * size * primal
        ),
        name="residuals",
    )(scale, *canon, *beside, ordered, handoff)


def share_kernel(inflow, out):
    total = inflow[0]
    for q in range(1, inflow.shape[0]):
        total = total + inflow[q]
    out[...] = jnp.broadcast_to(total[None], out.shape)


def shared_sum(inflow, copies):
    members, share, channels = inflow.shape
    return pl.pallas_call(
        share_kernel,
        out_shape=jax.ShapeDtypeStruct((copies, share, channels), F32),
        compiler_params=params(8),
        cost_estimate=cost(members * share * channels, 4 * (copies + members) * share * channels),
        name="shared_sum",
    )(inflow)


def local_kernel(slot, averaged, restore, mask, out):
    for d in range(averaged.shape[0]):
        s = slot[d]
        out[s] = (times(averaged[d], restore[d]) * mask[s]).astype(BF16)


def masked_local(slot, averaged, restore, mask):
    faces, samples, size = averaged.shape
    return pl.pallas_call(
        local_kernel,
        out_shape=pltpu.HBM(averaged.shape, BF16),
        grid_spec=pltpu.PrefetchScalarGridSpec(
            num_scalar_prefetch=1,
            grid=(1,),
            in_specs=[resident(averaged.shape), resident(restore.shape), resident(mask.shape)],
            out_specs=resident(averaged.shape),
        ),
        compiler_params=params(12),
        cost_estimate=cost(
            2 * faces * samples * size * size, 4 * faces * samples * size + 2 * faces * size * size
        ),
        name="masked_local",
    )(slot, in_hbm(averaged), in_hbm(restore), mask)


def dual_kernel(first, slot, scale, masked, sort, mask, inverse, out):
    d = first + pl.program_id(0)
    faces, _, size = masked.shape
    total = None
    for g in range(faces):
        term = times(masked[g], inverse[g * size : (g + 1) * size, :])
        total = term if total is None else total + term
    high, low = split(total * (mask[slot[d]] * scale[d]))
    out[0] = times(high, sort[0]) + times(low, sort[0])


def dual(first, count, slot, scale, masked, sort, mask, inverse):
    faces, samples, size = masked.shape
    return pl.pallas_call(
        functools.partial(dual_kernel, first),
        out_shape=pltpu.HBM((count, samples, size), F32),
        grid_spec=pltpu.PrefetchScalarGridSpec(
            num_scalar_prefetch=1,
            grid=(count,),
            in_specs=[
                pl.BlockSpec(memory_space=pltpu.SMEM),
                resident(masked.shape),
                pl.BlockSpec((1, size, size), lambda i, slot: (first + i, 0, 0)),
                resident(mask.shape),
                pl.BlockSpec((faces * size, size), lambda i, slot: (0, slot[first + i])),
            ],
            out_specs=pl.BlockSpec((1, samples, size), lambda i, slot: (i, 0, 0)),
        ),
        compiler_params=params(16),
        cost_estimate=cost(
            2 * count * samples * size * (faces + 2) * size,
            2 * count * size * (faces + 1) * size + 6 * faces * samples * size,
        ),
        name=f"dual{first}",
    )(slot, scale, in_hbm(masked), in_hbm(sort), mask, in_hbm(inverse))


DOUBLING = (4, 2, 1)
DOUBLED_BITS = (0, 4, 2, 6, 1, 5, 3, 7)
TINY = 1e-30


def triple(value, high, low):
    value_high, value_low = split(value)
    return times(value_high, high) + (times(value_low, high) + times(value_high, low))


def maps_kernel(transfer, maps, product):
    group, channels, _ = transfer.shape
    own = lax.rem(lax.axis_index("sub"), group)
    total = None
    for k in range(group):
        bits = jnp.bitwise_xor(own, k)
        place = (bits & 1) * 4 + (bits & 2) + lax.shift_right_logical(bits, 2)
        value = transfer[place]
        high, low = split(value)
        maps[2 * k] = high
        maps[2 * k + 1] = low
        largest = jnp.max(jnp.abs(value), axis=1, keepdims=True)
        largest = jnp.maximum(jnp.max(largest, axis=0, keepdims=True), TINY)
        product[0, pl.ds(channels + k, 1), :] = jnp.broadcast_to(largest, (1, channels))
        scaled = value / largest
        total = scaled if total is None else triple(total, *split(scaled))
    product[0, pl.ds(0, channels), :] = total


def group_maps(transfer):
    group, channels, _ = transfer.shape
    return pl.pallas_call(
        maps_kernel,
        out_shape=[
            pltpu.HBM((2 * group, channels, channels), BF16),
            jax.ShapeDtypeStruct((1, channels + group, channels), F32),
        ],
        grid=(1,),
        in_specs=[resident(transfer.shape)],
        out_specs=[
            resident((2 * group, channels, channels)),
            resident((1, channels + group, channels)),
        ],
        compiler_params=params(8),
        cost_estimate=cost(6 * group * channels**3, 8 * group * channels * channels),
        name="group_maps",
    )(transfer)


def run_lines(state, inflow, maps, count):
    def step(k, value):
        return triple(value, maps[2 * k], maps[2 * k + 1]) + inflow[k]

    return lax.fori_loop(0, count, step, state)


def outflow_kernel(inflow, maps, out):
    lines, samples, channels = inflow.shape
    state = jnp.zeros((samples, channels), F32)
    for k in range(lines):
        state = triple(state, maps[2 * k], maps[2 * k + 1]) + inflow[k] if k else inflow[0]
    out[...] = jnp.broadcast_to(state[None], out.shape)


def group_outflow(inflow, maps, copies):
    lines, samples, channels = inflow.shape
    return pl.pallas_call(
        outflow_kernel,
        out_shape=jax.ShapeDtypeStruct((copies, samples, channels), F32),
        grid=(1,),
        in_specs=[resident(inflow.shape), resident(maps.shape)],
        out_specs=IN_VMEM,
        compiler_params=params(8),
        cost_estimate=cost(
            6 * lines * samples * channels * channels, 4 * lines * channels * (samples + channels)
        ),
        name="group_outflow",
    )(inflow, in_hbm(maps))


def carried_kernel(outflow, products, inflow, maps, out):
    lines, samples, channels = inflow.shape
    line = lax.axis_index("sub")
    group = lax.div(line, lines)

    def enter(a, value):
        place = jnp.bitwise_xor(group, a)
        value = triple(value, *split(products[place, pl.ds(0, channels), :]))
        for k in range(lines):
            value = value * products[place, pl.ds(channels + k, 1), :]
        return value + outflow[a]

    state = lax.fori_loop(0, group, enter, jnp.zeros((samples, channels), F32))
    state = run_lines(state, inflow, maps, lax.rem(line, lines))
    out[...] = jnp.broadcast_to(state[None], out.shape)


def carried_states(outflow, products, inflow, maps, copies):
    lines, samples, channels = inflow.shape
    return pl.pallas_call(
        carried_kernel,
        out_shape=jax.ShapeDtypeStruct((copies, samples, channels), F32),
        grid=(1,),
        in_specs=[
            resident(outflow.shape),
            resident(products.shape),
            resident(inflow.shape),
            resident(maps.shape),
        ],
        out_specs=IN_VMEM,
        compiler_params=params(8),
        cost_estimate=cost(
            6 * lines * samples * channels * channels, 8 * lines * channels * (samples + channels)
        ),
        name="carried_states",
    )(outflow, products, inflow, in_hbm(maps))


def line_kernel(gathered, inverse, out):
    members, _, primal = gathered.shape
    member = lax.axis_index("coarse")
    total = None
    for i, bits in enumerate(GATHER_BITS):
        start = pl.multiple_of(jnp.bitwise_xor(member, bits) * primal, primal)
        term = times(gathered[i], inverse[pl.ds(start, primal), :])
        total = term if total is None else total + term
    out[...] = total


def line_base(gathered, inverse):
    members, samples, primal = gathered.shape
    return pl.pallas_call(
        line_kernel,
        out_shape=jax.ShapeDtypeStruct((samples, primal), F32),
        grid=(1,),
        in_specs=[resident(gathered.shape), resident(inverse.shape)],
        out_specs=IN_VMEM,
        compiler_params=params(12),
        cost_estimate=cost(
            2 * members * samples * primal * primal, 2 * members * primal * (samples + primal)
        ),
        name="line_base",
    )(gathered, in_hbm(inverse))


def extend_kernel(scale, base, carried, coupling, ordered_columns, dual0, dual1, *rest):
    outs, answer = rest[:-1], rest[-1]
    d = pl.program_id(0)

    @pl.when(d == 0)
    def _():
        high, low = split(carried[...])
        term = times(high, coupling[...]) + times(low, coupling[...])
        answer[...] = (base[...] + term).astype(BF16)

    value = scale[d] * times(answer[...], ordered_columns[0])
    half = len(outs) // 2
    for i, out in enumerate(outs):

        @pl.when(d == i)
        def _():
            out[...] = ((dual0 if i < half else dual1)[0] + value).astype(BF16)


def extend(scale, base, carried, coupling, ordered_columns, dual0, dual1):
    half, samples, size = dual0.shape
    faces = 2 * half
    primal = base.shape[1]
    channels = carried.shape[1]
    return pl.pallas_call(
        extend_kernel,
        out_shape=[jax.ShapeDtypeStruct((samples, size), BF16)] * faces,
        grid=(faces,),
        in_specs=[
            pl.BlockSpec(memory_space=pltpu.SMEM),
            IN_VMEM,
            IN_VMEM,
            resident((channels, primal)),
            pl.BlockSpec((1, primal, size), lambda d: (d, 0, 0)),
            pl.BlockSpec((1, samples, size), lambda d: (jnp.minimum(d, half - 1), 0, 0)),
            pl.BlockSpec((1, samples, size), lambda d: (jnp.maximum(d - half, 0), 0, 0)),
        ],
        out_specs=[IN_VMEM] * faces,
        scratch_shapes=[pltpu.VMEM((samples, primal), BF16)],
        compiler_params=params(8),
        cost_estimate=cost(
            2 * faces * samples * size * primal, 6 * faces * samples * size + 2 * faces * size * primal
        ),
        name="extend",
    )(scale, base, carried, in_hbm(coupling), in_hbm(ordered_columns), in_hbm(dual0), in_hbm(dual1))


def finish_kernel(slot, *refs):
    d = pl.program_id(0)
    restore, out = refs[-2:]
    faces = (len(refs) - 2) // 2
    for i in range(faces):

        @pl.when(d == i)
        def _():
            value = sum_across(refs[i], refs[faces + i], i).astype(BF16)
            out[0] = times(value, restore[i]).astype(BF16)


def finish(slot, weighted, beside, restore):
    faces, size, _ = restore.shape
    samples = weighted[0].shape[0]
    return pl.pallas_call(
        finish_kernel,
        out_shape=jax.ShapeDtypeStruct((faces, samples, size), BF16),
        grid_spec=pltpu.PrefetchScalarGridSpec(
            num_scalar_prefetch=1,
            grid=(faces,),
            in_specs=[IN_VMEM] * (2 * faces + 1),
            out_specs=pl.BlockSpec((1, samples, size), lambda d, s: (s[d], 0, 0)),
        ),
        compiler_params=params(8),
        cost_estimate=cost(
            2 * faces * samples * size * size, 6 * faces * samples * size + 2 * faces * size * size
        ),
        name="finish",
    )(slot, *weighted, *beside, restore)


GROUP = 8
GATHER_STAGES = (2, 1, 4)
GATHER_BITS = (0, 2, 1, 3, 4, 6, 5, 7)


def exchange(value, axis, bit):
    return lax.ppermute(value, axis, [(i, i ^ bit) for i in range(lax.axis_size(axis))])


def doubled(value, axis, bit):
    return jnp.concatenate([value, exchange(value, axis, bit)])


def neighbours(faces):
    lower, upper, left, right = faces

    def shifted(value, axis, step):
        count = lax.axis_size(axis)
        pairs = [(i, (i + step) % count) for i in range(count)]
        return lax.ppermute(value, axis, pairs)

    return (
        shifted(upper, "sub", 1),
        shifted(lower, "sub", -1),
        shifted(right, "coarse", 1),
        shifted(left, "coarse", -1),
    )


def per_device(
    residual_parts,
    face_slot,
    face_order,
    face_scale,
    vertex_unknowns,
    front_inverse,
    coarse_basis,
    coarse_inverse,
    thermal_handoff,
    chain_transfer,
    coupling_in,
):
    parts = residual_parts[0, 0]
    slot = face_slot[0, 0]
    order = face_order[0, 0]
    scale = face_scale[0, 0]
    faces, samples, size = parts.shape
    basis = coarse_basis[0, 0].reshape(faces, size, -1)
    lines, members = lax.axis_size("sub"), lax.axis_size("coarse")
    share = samples // members

    groups = lines // GROUP
    inside = [[a * GROUP + b for b in range(GROUP)] for a in range(groups)]
    between = [[a * GROUP + b for a in range(groups)] for b in range(GROUP)]
    transfer = chain_transfer
    for bit in DOUBLING:
        transfer = doubled(transfer, "sub", bit)

    canon = to_canonical(slot, parts, order)
    beside = neighbours(canon)
    basis, canon = lax.optimization_barrier((basis, canon))
    sort, restore, ordered, ordered_columns = tables(slot, order, basis)
    averaged, coarse_residual, heat = residuals(
        scale, canon, beside, ordered, thermal_handoff[0]
    )
    positions = lax.broadcasted_iota(jnp.int32, (vertex_unknowns.shape[2], faces * size), 1)
    hits = jnp.sum((vertex_unknowns[0, 0][:, None] == positions).astype(F32), axis=0)
    mask = (1.0 - hits).reshape(faces, 1, size)

    channels = heat.shape[1]
    gathered = coarse_residual[None]
    received = exchange(gathered, "coarse", GATHER_STAGES[0])
    inflow = lax.all_to_all(heat.reshape(members, share, channels), "coarse", 0, 0)
    masked = masked_local(slot, averaged, restore, mask)
    inflow, masked = lax.optimization_barrier((inflow, masked))
    inflow = shared_sum(inflow, GROUP)
    masked, inflow = lax.optimization_barrier((masked, inflow))

    inflow = lax.all_to_all(inflow, "sub", 0, 0, axis_index_groups=inside)
    half = faces // 2
    dual0 = dual(0, half, slot, scale, masked, sort, mask, front_inverse[0, 0])
    transfer, received, dual0 = lax.optimization_barrier((transfer, received, dual0))
    maps, product = group_maps(transfer)
    others = exchange(product, "sub", GROUP)
    gathered = jnp.concatenate([gathered, received])
    received = exchange(gathered, "coarse", GATHER_STAGES[1])
    inflow, maps, masked = lax.optimization_barrier((inflow, maps, masked))

    outflow = group_outflow(inflow, maps, groups)
    masked, others, outflow = lax.optimization_barrier((masked, others, outflow))
    outflow = lax.all_to_all(outflow, "sub", 0, 0, axis_index_groups=between)
    product = jnp.concatenate([product, others])
    others = exchange(product, "sub", 2 * GROUP)
    dual1 = dual(half, half, slot, scale, masked, sort, mask, front_inverse[0, 0])
    outflow, others, received, dual1 = lax.optimization_barrier((outflow, others, received, dual1))
    product = jnp.concatenate([product, others])
    gathered = jnp.concatenate([gathered, received])
    gathered = doubled(gathered, "coarse", GATHER_STAGES[2])
    carried = carried_states(outflow, product, inflow, maps, members)
    carried = lax.all_to_all(carried, "coarse", 0, 0).reshape(samples, channels)
    base = line_base(gathered, coarse_inverse[0])

    weighted = extend(scale, base, carried, coupling_in[0], ordered_columns, dual0, dual1)
    beside = neighbours(weighted)
    return finish(slot, weighted, beside, restore)[None, None]


def solution(mesh):
    placed = (
        P("sub", "coarse", None, None, None),
        P("sub", "coarse", None),
        P("sub", "coarse", None, None),
        P("sub", "coarse", None),
        P("sub", "coarse", None),
        P("sub", "coarse", None, None),
        P("sub", "coarse", None, None),
        P("sub", None, "coarse"),
        P("sub", None, None),
        P("sub", None, None),
        P("sub", None, "coarse"),
    )
    return jax.shard_map(
        per_device,
        mesh=mesh,
        in_specs=placed,
        out_specs=P("sub", "coarse", None, None, None),
        check_vma=False,
    )
```

```python
import functools

import jax
import jax.numpy as jnp
from jax import lax
from jax.experimental import pallas as pl
from jax.experimental.pallas import tpu as pltpu
from jax.sharding import PartitionSpec as P

BF16 = jnp.bfloat16
F32 = jnp.float32


def params(megabytes):
    return pltpu.CompilerParams(vmem_limit_bytes=megabytes << 20)


def cost(flops, bytes_accessed):
    return pl.CostEstimate(flops=flops, bytes_accessed=bytes_accessed, transcendentals=0)


def resident(shape):
    return pl.BlockSpec(shape, lambda *_: (0,) * len(shape))


IN_VMEM = pl.BlockSpec(memory_space=pltpu.VMEM)


def in_hbm(value):
    return pltpu.with_memory_space_constraint(value, pltpu.HBM)


def times(a, b):
    return jnp.dot(a, b, preferred_element_type=F32)


def times_columns(a, b):
    return lax.dot_general(a, b, (((0,), (0,)), ((), ())), preferred_element_type=F32)


def split(value):
    high = value.astype(BF16)
    return high, (value - high.astype(F32)).astype(BF16)


def sorting_table(order, face):
    size = order.shape[1]
    local = lax.broadcasted_iota(jnp.int32, (size, size), 0)
    return jnp.where(local == order[pl.ds(face, 1), :], 1.0, 0.0)


def canon_kernel(slot, parts, order, *outs):
    d = pl.program_id(0)
    table = sorting_table(order, slot[d]).astype(BF16)
    value = times(parts[0], table).astype(BF16)
    for i, out in enumerate(outs):

        @pl.when(d == i)
        def _():
            out[...] = value


def to_canonical(slot, parts, order):
    faces, samples, size = parts.shape
    return pl.pallas_call(
        canon_kernel,
        out_shape=[jax.ShapeDtypeStruct((samples, size), BF16)] * faces,
        grid_spec=pltpu.PrefetchScalarGridSpec(
            num_scalar_prefetch=1,
            grid=(faces,),
            in_specs=[
                pl.BlockSpec((1, samples, size), lambda d, slot: (slot[d], 0, 0)),
                resident((faces, size)),
            ],
            out_specs=[IN_VMEM] * faces,
        ),
        compiler_params=params(8),
        cost_estimate=cost(2 * faces * samples * size * size, 4 * faces * samples * size),
        name="canon",
    )(slot, in_hbm(parts), in_hbm(order))


def tables_kernel(slot, order, basis, sort, restore, ordered, ordered_columns):
    d = pl.program_id(0)
    table = sorting_table(order, slot[d])
    sort[0] = table.astype(BF16)
    restore[0] = table.T.astype(BF16)
    ordered[0] = times(restore[0], basis[0]).astype(BF16)
    ordered_columns[0] = times_columns(basis[0], sort[0]).astype(BF16)


def tables(slot, order, basis):
    faces, size, primal = basis.shape

    def by_direction(*shape):
        return pl.BlockSpec((1,) + shape, lambda d, slot: (d, 0, 0))

    return pl.pallas_call(
        tables_kernel,
        out_shape=[
            pltpu.HBM((faces, size, size), BF16),
            pltpu.HBM((faces, size, size), BF16),
            jax.ShapeDtypeStruct((faces, size, primal), BF16),
            pltpu.HBM((faces, primal, size), BF16),
        ],
        grid_spec=pltpu.PrefetchScalarGridSpec(
            num_scalar_prefetch=1,
            grid=(faces,),
            in_specs=[
                resident((faces, size)),
                pl.BlockSpec((1, size, primal), lambda d, slot: (slot[d], 0, 0)),
            ],
            out_specs=[
                by_direction(size, size),
                by_direction(size, size),
                by_direction(size, primal),
                by_direction(primal, size),
            ],
        ),
        compiler_params=params(12),
        cost_estimate=cost(
            4 * faces * size * size * primal, 4 * faces * size * size + 6 * faces * size * primal
        ),
        name="tables",
    )(slot, in_hbm(order), in_hbm(basis))


def has_neighbour(d):
    axis = "sub" if d < 2 else "coarse"
    place = lax.axis_index(axis)
    return place > 0 if d % 2 == 0 else place < lax.axis_size(axis) - 1


def sum_across(own, beside, d):
    own, beside = own[...].astype(F32), beside[...].astype(F32)
    return own + jnp.where(has_neighbour(d), beside, 0.0)


def residual_kernel(scale, *refs):
    faces = scale.shape[0]
    canon, beside = refs[:faces], refs[faces : 2 * faces]
    ordered, handoff, averaged, coarse, heat = refs[2 * faces :]
    total = None
    for d in range(faces):
        value = (scale[d] * sum_across(canon[d], beside[d], d)).astype(BF16)
        averaged[d] = value
        term = times(value, ordered[d])
        total = term if total is None else total + term
    rounded = total.astype(BF16)
    coarse[...] = rounded
    primal = rounded.shape[1]
    start = pl.multiple_of(lax.axis_index("coarse") * primal, primal)
    heat[...] = times(rounded, handoff[pl.ds(start, primal), :])


def residuals(scale, canon, beside, ordered, handoff):
    faces, size, primal = ordered.shape
    samples = canon[0].shape[0]
    channels = handoff.shape[1]
    return pl.pallas_call(
        residual_kernel,
        out_shape=[
            pltpu.HBM((faces, samples, size), BF16),
            jax.ShapeDtypeStruct((samples, primal), BF16),
            jax.ShapeDtypeStruct((samples, channels), F32),
        ],
        grid=(1,),
        in_specs=[pl.BlockSpec(memory_space=pltpu.SMEM)] + [IN_VMEM] * (2 * faces + 2),
        out_specs=[resident((faces, samples, size)), IN_VMEM, IN_VMEM],
        compiler_params=params(8),
        cost_estimate=cost(
            2 * faces * samples * size * primal, 6 * faces * samples * size + 2 * faces * size * primal
        ),
        name="residuals",
    )(scale, *canon, *beside, ordered, handoff)


def share_kernel(inflow, out):
    total = inflow[0]
    for q in range(1, inflow.shape[0]):
        total = total + inflow[q]
    out[...] = jnp.broadcast_to(total[None], out.shape)


def shared_sum(inflow, copies):
    members, share, channels = inflow.shape
    return pl.pallas_call(
        share_kernel,
        out_shape=jax.ShapeDtypeStruct((copies, share, channels), F32),
        compiler_params=params(8),
        cost_estimate=cost(members * share * channels, 4 * (copies + members) * share * channels),
        name="shared_sum",
    )(inflow)


def local_kernel(slot, averaged, restore, mask, out):
    for d in range(averaged.shape[0]):
        s = slot[d]
        out[s] = (times(averaged[d], restore[d]) * mask[s]).astype(BF16)


def masked_local(slot, averaged, restore, mask):
    faces, samples, size = averaged.shape
    return pl.pallas_call(
        local_kernel,
        out_shape=pltpu.HBM(averaged.shape, BF16),
        grid_spec=pltpu.PrefetchScalarGridSpec(
            num_scalar_prefetch=1,
            grid=(1,),
            in_specs=[resident(averaged.shape), resident(restore.shape), resident(mask.shape)],
            out_specs=resident(averaged.shape),
        ),
        compiler_params=params(12),
        cost_estimate=cost(
            2 * faces * samples * size * size, 4 * faces * samples * size + 2 * faces * size * size
        ),
        name="masked_local",
    )(slot, in_hbm(averaged), in_hbm(restore), mask)


def dual_kernel(first, slot, scale, masked, sort, mask, inverse, out):
    d = first + pl.program_id(0)
    faces, _, size = masked.shape
    total = None
    for g in range(faces):
        term = times(masked[g], inverse[g * size : (g + 1) * size, :])
        total = term if total is None else total + term
    high, low = split(total * (mask[slot[d]] * scale[d]))
    out[0] = times(high, sort[0]) + times(low, sort[0])


def dual(first, count, slot, scale, masked, sort, mask, inverse):
    faces, samples, size = masked.shape
    return pl.pallas_call(
        functools.partial(dual_kernel, first),
        out_shape=pltpu.HBM((count, samples, size), F32),
        grid_spec=pltpu.PrefetchScalarGridSpec(
            num_scalar_prefetch=1,
            grid=(count,),
            in_specs=[
                pl.BlockSpec(memory_space=pltpu.SMEM),
                resident(masked.shape),
                pl.BlockSpec((1, size, size), lambda i, slot: (first + i, 0, 0)),
                resident(mask.shape),
                pl.BlockSpec((faces * size, size), lambda i, slot: (0, slot[first + i])),
            ],
            out_specs=pl.BlockSpec((1, samples, size), lambda i, slot: (i, 0, 0)),
        ),
        compiler_params=params(16),
        cost_estimate=cost(
            2 * count * samples * size * (faces + 2) * size,
            2 * count * size * (faces + 1) * size + 6 * faces * samples * size,
        ),
        name=f"dual{first}",
    )(slot, scale, in_hbm(masked), in_hbm(sort), mask, in_hbm(inverse))


DOUBLING = (4, 2, 1)
DOUBLED_BITS = (0, 4, 2, 6, 1, 5, 3, 7)
TINY = 1e-30


def triple(value, high, low):
    value_high, value_low = split(value)
    return times(value_high, high) + (times(value_low, high) + times(value_high, low))


def maps_kernel(transfer, maps, product):
    group, channels, _ = transfer.shape
    own = lax.rem(lax.axis_index("sub"), group)
    total = None
    for k in range(group):
        bits = jnp.bitwise_xor(own, k)
        place = (bits & 1) * 4 + (bits & 2) + lax.shift_right_logical(bits, 2)
        value = transfer[place]
        high, low = split(value)
        maps[2 * k] = high
        maps[2 * k + 1] = low
        largest = jnp.max(jnp.abs(value), axis=1, keepdims=True)
        largest = jnp.maximum(jnp.max(largest, axis=0, keepdims=True), TINY)
        product[0, pl.ds(channels + k, 1), :] = jnp.broadcast_to(largest, (1, channels))
        scaled = value / largest
        total = scaled if total is None else triple(total, *split(scaled))
    product[0, pl.ds(0, channels), :] = total


def group_maps(transfer):
    group, channels, _ = transfer.shape
    return pl.pallas_call(
        maps_kernel,
        out_shape=[
            pltpu.HBM((2 * group, channels, channels), BF16),
            jax.ShapeDtypeStruct((1, channels + group, channels), F32),
        ],
        grid=(1,),
        in_specs=[resident(transfer.shape)],
        out_specs=[
            resident((2 * group, channels, channels)),
            resident((1, channels + group, channels)),
        ],
        compiler_params=params(8),
        cost_estimate=cost(6 * group * channels**3, 8 * group * channels * channels),
        name="group_maps",
    )(transfer)


def run_lines(state, inflow, maps, count):
    def step(k, value):
        return triple(value, maps[2 * k], maps[2 * k + 1]) + inflow[k]

    return lax.fori_loop(0, count, step, state)


def outflow_kernel(inflow, maps, out):
    lines, samples, channels = inflow.shape
    state = jnp.zeros((samples, channels), F32)
    for k in range(lines):
        state = triple(state, maps[2 * k], maps[2 * k + 1]) + inflow[k] if k else inflow[0]
    out[...] = state


def group_outflow(inflow, maps):
    lines, samples, channels = inflow.shape
    return pl.pallas_call(
        outflow_kernel,
        out_shape=jax.ShapeDtypeStruct((samples, channels), F32),
        grid=(1,),
        in_specs=[resident(inflow.shape), resident(maps.shape)],
        out_specs=IN_VMEM,
        compiler_params=params(8),
        cost_estimate=cost(
            6 * lines * samples * channels * channels, 4 * lines * channels * (samples + channels)
        ),
        name="group_outflow",
    )(inflow, in_hbm(maps))


def carried_kernel(products, inflow, maps, *refs):
    outflows, out = refs[:-1], refs[-1]
    lines, samples, channels = inflow.shape
    line = lax.axis_index("sub")
    group = lax.div(line, lines)
    state = jnp.zeros((samples, channels), F32)
    for step, outflow in zip(range(len(outflows), 0, -1), outflows):
        place = jnp.bitwise_xor(group, jnp.maximum(group - step, 0))
        value = triple(state, *split(products[place, pl.ds(0, channels), :]))
        for k in range(lines):
            value = value * products[place, pl.ds(channels + k, 1), :]
        state = jnp.where(group >= step, value + outflow[...], state)
    state = run_lines(state, inflow, maps, lax.rem(line, lines))
    out[...] = jnp.broadcast_to(state[None], out.shape)


def carried_states(outflows, products, inflow, maps, copies):
    lines, samples, channels = inflow.shape
    return pl.pallas_call(
        carried_kernel,
        out_shape=jax.ShapeDtypeStruct((copies, samples, channels), F32),
        grid=(1,),
        in_specs=[
            resident(products.shape),
            resident(inflow.shape),
            resident(maps.shape),
        ]
        + [resident((samples, channels))] * len(outflows),
        out_specs=IN_VMEM,
        compiler_params=params(8),
        cost_estimate=cost(
            6 * lines * samples * channels * channels, 8 * lines * channels * (samples + channels)
        ),
        name="carried_states",
    )(products, inflow, in_hbm(maps), *outflows)


def line_kernel(gathered, inverse, out):
    members, _, primal = gathered.shape
    member = lax.axis_index("coarse")
    total = None
    for i, bits in enumerate(GATHER_BITS):
        start = pl.multiple_of(jnp.bitwise_xor(member, bits) * primal, primal)
        term = times(gathered[i], inverse[pl.ds(start, primal), :])
        total = term if total is None else total + term
    out[...] = total


def line_base(gathered, inverse):
    members, samples, primal = gathered.shape
    return pl.pallas_call(
        line_kernel,
        out_shape=jax.ShapeDtypeStruct((samples, primal), F32),
        grid=(1,),
        in_specs=[resident(gathered.shape), resident(inverse.shape)],
        out_specs=IN_VMEM,
        compiler_params=params(12),
        cost_estimate=cost(
            2 * members * samples * primal * primal, 2 * members * primal * (samples + primal)
        ),
        name="line_base",
    )(gathered, in_hbm(inverse))


def extend_kernel(scale, base, carried, coupling, ordered_columns, dual0, dual1, *outs):
    high, low = split(carried[...])
    term = times(high, coupling[...]) + times(low, coupling[...])
    answer = (base[...] + term).astype(BF16)
    half = len(outs) // 2
    for d, out in enumerate(outs):
        value = dual0[d] if d < half else dual1[d - half]
        out[...] = (value + scale[d] * times(answer, ordered_columns[d])).astype(BF16)


def extend(scale, base, carried, coupling, ordered_columns, dual0, dual1):
    half, samples, size = dual0.shape
    faces = 2 * half
    primal = base.shape[1]
    return pl.pallas_call(
        extend_kernel,
        out_shape=[jax.ShapeDtypeStruct((samples, size), BF16)] * faces,
        grid=(1,),
        in_specs=[
            pl.BlockSpec(memory_space=pltpu.SMEM),
            IN_VMEM,
            IN_VMEM,
            resident(coupling.shape),
            resident(ordered_columns.shape),
            resident(dual0.shape),
            resident(dual1.shape),
        ],
        out_specs=[IN_VMEM] * faces,
        compiler_params=params(12),
        cost_estimate=cost(
            2 * faces * samples * size * primal, 6 * faces * samples * size + 2 * faces * size * primal
        ),
        name="extend",
    )(scale, base, carried, in_hbm(coupling), in_hbm(ordered_columns), in_hbm(dual0), in_hbm(dual1))


def finish_kernel(slot, *refs):
    d = pl.program_id(0)
    restore, out = refs[-2:]
    faces = (len(refs) - 2) // 2
    for i in range(faces):

        @pl.when(d == i)
        def _():
            value = sum_across(refs[i], refs[faces + i], i).astype(BF16)
            out[0] = times(value, restore[i]).astype(BF16)


def finish(slot, weighted, beside, restore):
    faces, size, _ = restore.shape
    samples = weighted[0].shape[0]
    return pl.pallas_call(
        finish_kernel,
        out_shape=jax.ShapeDtypeStruct((faces, samples, size), BF16),
        grid_spec=pltpu.PrefetchScalarGridSpec(
            num_scalar_prefetch=1,
            grid=(faces,),
            in_specs=[IN_VMEM] * (2 * faces + 1),
            out_specs=pl.BlockSpec((1, samples, size), lambda d, s: (s[d], 0, 0)),
        ),
        compiler_params=params(8),
        cost_estimate=cost(
            2 * faces * samples * size * size, 6 * faces * samples * size + 2 * faces * size * size
        ),
        name="finish",
    )(slot, *weighted, *beside, restore)


GROUP = 8
GATHER_STAGES = (2, 1, 4)
GATHER_BITS = (0, 2, 1, 3, 4, 6, 5, 7)


def exchange(value, axis, bit):
    return lax.ppermute(value, axis, [(i, i ^ bit) for i in range(lax.axis_size(axis))])


def doubled(value, axis, bit):
    return jnp.concatenate([value, exchange(value, axis, bit)])


def shifted(value, axis, step):
    count = lax.axis_size(axis)
    return lax.ppermute(value, axis, [(i, (i + step) % count) for i in range(count)])


def neighbours(faces):
    lower, upper, left, right = faces
    return (
        shifted(upper, "sub", 1),
        shifted(lower, "sub", -1),
        shifted(right, "coarse", 1),
        shifted(left, "coarse", -1),
    )


def per_device(
    residual_parts,
    face_slot,
    face_order,
    face_scale,
    vertex_unknowns,
    front_inverse,
    coarse_basis,
    coarse_inverse,
    thermal_handoff,
    chain_transfer,
    coupling_in,
):
    parts = residual_parts[0, 0]
    slot = face_slot[0, 0]
    order = face_order[0, 0]
    scale = face_scale[0, 0]
    faces, samples, size = parts.shape
    basis = coarse_basis[0, 0].reshape(faces, size, -1)
    lines, members = lax.axis_size("sub"), lax.axis_size("coarse")
    share = samples // members

    groups = lines // GROUP
    inside = [[a * GROUP + b for b in range(GROUP)] for a in range(groups)]
    copied = exchange(chain_transfer, "sub", DOUBLING[0])

    canon = to_canonical(slot, parts, order)
    copied, canon = lax.optimization_barrier((copied, canon))
    transfer = jnp.concatenate([chain_transfer, copied])
    copied = exchange(transfer, "sub", DOUBLING[1])
    beside = neighbours(canon)
    basis, canon = lax.optimization_barrier((basis, canon))
    sort, restore, ordered, ordered_columns = tables(slot, order, basis)
    averaged, coarse_residual, heat = residuals(
        scale, canon, beside, ordered, thermal_handoff[0]
    )
    copied, heat = lax.optimization_barrier((copied, heat))
    transfer = doubled(jnp.concatenate([transfer, copied]), "sub", DOUBLING[2])
    positions = lax.broadcasted_iota(jnp.int32, (vertex_unknowns.shape[2], faces * size), 1)
    hits = jnp.sum((vertex_unknowns[0, 0][:, None] == positions).astype(F32), axis=0)
    mask = (1.0 - hits).reshape(faces, 1, size)

    channels = heat.shape[1]
    gathered = coarse_residual[None]
    received = exchange(gathered, "coarse", GATHER_STAGES[0])
    inflow = lax.all_to_all(heat.reshape(members, share, channels), "coarse", 0, 0)
    masked = masked_local(slot, averaged, restore, mask)
    inflow, masked = lax.optimization_barrier((inflow, masked))
    inflow = shared_sum(inflow, GROUP)
    masked, transfer, received, inflow = lax.optimization_barrier((masked, transfer, received, inflow))

    inflow = lax.all_to_all(inflow, "sub", 0, 0, axis_index_groups=inside)
    half = faces // 2
    dual0 = dual(0, half, slot, scale, masked, sort, mask, front_inverse[0, 0])
    transfer, dual0 = lax.optimization_barrier((transfer, dual0))
    maps, product = group_maps(transfer)
    others = exchange(product, "sub", GROUP)
    gathered = jnp.concatenate([gathered, received])
    received = exchange(gathered, "coarse", GATHER_STAGES[1])
    inflow, maps, masked = lax.optimization_barrier((inflow, maps, masked))

    outflow = group_outflow(inflow, maps)
    masked, others, received, outflow = lax.optimization_barrier((masked, others, received, outflow))
    outflows = [shifted(outflow, "sub", GROUP * step) for step in range(groups - 1, 0, -1)]
    product = jnp.concatenate([product, others])
    others = exchange(product, "sub", 2 * GROUP)
    gathered = jnp.concatenate([gathered, received])
    masked, gathered = lax.optimization_barrier((masked, gathered))
    dual1 = dual(half, half, slot, scale, masked, sort, mask, front_inverse[0, 0])
    received = exchange(gathered, "coarse", GATHER_STAGES[2])
    outflows, others, dual1 = lax.optimization_barrier((outflows, others, dual1))
    product = jnp.concatenate([product, others])
    gathered = jnp.concatenate([gathered, received])
    carried = carried_states(outflows, product, inflow, maps, members)
    carried = lax.all_to_all(carried, "coarse", 0, 0).reshape(samples, channels)
    base = line_base(gathered, coarse_inverse[0])

    weighted = extend(scale, base, carried, coupling_in[0], ordered_columns, dual0, dual1)
    beside = neighbours(weighted)
    return finish(slot, weighted, beside, restore)[None, None]


def solution(mesh):
    placed = (
        P("sub", "coarse", None, None, None),
        P("sub", "coarse", None),
        P("sub", "coarse", None, None),
        P("sub", "coarse", None),
        P("sub", "coarse", None),
        P("sub", "coarse", None, None),
        P("sub", "coarse", None, None),
        P("sub", None, "coarse"),
        P("sub", None, None),
        P("sub", None, None),
        P("sub", None, "coarse"),
    )
    return jax.shard_map(
        per_device,
        mesh=mesh,
        in_specs=placed,
        out_specs=P("sub", "coarse", None, None, None),
        check_vma=False,
    )
```

```python
import functools

import jax
import jax.numpy as jnp
from jax import lax
from jax.experimental import pallas as pl
from jax.experimental.pallas import tpu as pltpu
from jax.sharding import PartitionSpec as P

BF16 = jnp.bfloat16
F32 = jnp.float32


def params(megabytes):
    return pltpu.CompilerParams(vmem_limit_bytes=megabytes << 20)


def cost(flops, bytes_accessed):
    return pl.CostEstimate(flops=flops, bytes_accessed=bytes_accessed, transcendentals=0)


def resident(shape):
    return pl.BlockSpec(shape, lambda *_: (0,) * len(shape))


IN_VMEM = pl.BlockSpec(memory_space=pltpu.VMEM)


def in_hbm(value):
    return pltpu.with_memory_space_constraint(value, pltpu.HBM)


def times(a, b):
    return jnp.dot(a, b, preferred_element_type=F32)


def times_columns(a, b):
    return lax.dot_general(a, b, (((0,), (0,)), ((), ())), preferred_element_type=F32)


def split(value):
    high = value.astype(BF16)
    return high, (value - high.astype(F32)).astype(BF16)


def sorting_table(order, face):
    size = order.shape[1]
    local = lax.broadcasted_iota(jnp.int32, (size, size), 0)
    return jnp.where(local == order[pl.ds(face, 1), :], 1.0, 0.0)


def canon_kernel(slot, parts, order, *outs):
    for d, out in enumerate(outs):
        s = slot[d]
        out[...] = times(parts[s], sorting_table(order, s).astype(BF16)).astype(BF16)


def to_canonical(slot, parts, order):
    faces, samples, size = parts.shape
    return pl.pallas_call(
        canon_kernel,
        out_shape=[jax.ShapeDtypeStruct((samples, size), BF16)] * faces,
        grid_spec=pltpu.PrefetchScalarGridSpec(
            num_scalar_prefetch=1,
            grid=(1,),
            in_specs=[resident(parts.shape), resident((faces, size))],
            out_specs=[IN_VMEM] * faces,
        ),
        compiler_params=params(8),
        cost_estimate=cost(2 * faces * samples * size * size, 4 * faces * samples * size),
        name="canon",
    )(slot, in_hbm(parts), in_hbm(order))


def tables_kernel(slot, order, basis, sort, restore, restore_near, ordered, ordered_columns):
    d = pl.program_id(0)
    table = sorting_table(order, slot[d])
    sort[0] = table.astype(BF16)
    restore[0] = table.T.astype(BF16)
    restore_near[0] = restore[0]
    ordered[0] = times(restore[0], basis[0]).astype(BF16)
    ordered_columns[0] = times_columns(basis[0], sort[0]).astype(BF16)


def tables(slot, order, basis):
    faces, size, primal = basis.shape

    def by_direction(*shape):
        return pl.BlockSpec((1,) + shape, lambda d, slot: (d, 0, 0))

    return pl.pallas_call(
        tables_kernel,
        out_shape=[
            pltpu.HBM((faces, size, size), BF16),
            pltpu.HBM((faces, size, size), BF16),
            jax.ShapeDtypeStruct((faces, size, size), BF16),
            jax.ShapeDtypeStruct((faces, size, primal), BF16),
            pltpu.HBM((faces, primal, size), BF16),
        ],
        grid_spec=pltpu.PrefetchScalarGridSpec(
            num_scalar_prefetch=1,
            grid=(faces,),
            in_specs=[
                resident((faces, size)),
                pl.BlockSpec((1, size, primal), lambda d, slot: (slot[d], 0, 0)),
            ],
            out_specs=[
                by_direction(size, size),
                by_direction(size, size),
                by_direction(size, size),
                by_direction(size, primal),
                by_direction(primal, size),
            ],
        ),
        compiler_params=params(12),
        cost_estimate=cost(
            4 * faces * size * size * primal, 4 * faces * size * size + 6 * faces * size * primal
        ),
        name="tables",
    )(slot, in_hbm(order), in_hbm(basis))


def has_neighbour(d):
    axis = "sub" if d < 2 else "coarse"
    place = lax.axis_index(axis)
    return place > 0 if d % 2 == 0 else place < lax.axis_size(axis) - 1


def sum_across(own, beside, d):
    own, beside = own[...].astype(F32), beside[...].astype(F32)
    return own + jnp.where(has_neighbour(d), beside, 0.0)


def residual_kernel(slot, scale, *refs):
    faces = scale.shape[0]
    canon, beside = refs[:faces], refs[faces : 2 * faces]
    ordered, restore, handoff, mask, masked, coarse, heat = refs[2 * faces :]
    total = None
    for d in range(faces):
        value = (scale[d] * sum_across(canon[d], beside[d], d)).astype(BF16)
        term = times(value, ordered[d])
        total = term if total is None else total + term
        s = slot[d]
        masked[s] = (times(value, restore[d]) * mask[s]).astype(BF16)
    rounded = total.astype(BF16)
    coarse[...] = rounded
    primal = rounded.shape[1]
    start = pl.multiple_of(lax.axis_index("coarse") * primal, primal)
    heat[...] = times(rounded, handoff[pl.ds(start, primal), :])


def residuals(slot, scale, canon, beside, ordered, restore, handoff, mask):
    faces, size, primal = ordered.shape
    samples = canon[0].shape[0]
    channels = handoff.shape[1]
    return pl.pallas_call(
        residual_kernel,
        out_shape=[
            pltpu.HBM((faces, samples, size), BF16),
            jax.ShapeDtypeStruct((samples, primal), BF16),
            jax.ShapeDtypeStruct((samples, channels), F32),
        ],
        grid_spec=pltpu.PrefetchScalarGridSpec(
            num_scalar_prefetch=1,
            grid=(1,),
            in_specs=[pl.BlockSpec(memory_space=pltpu.SMEM)] + [IN_VMEM] * (2 * faces + 4),
            out_specs=[resident((faces, samples, size)), IN_VMEM, IN_VMEM],
        ),
        compiler_params=params(8),
        cost_estimate=cost(
            2 * faces * samples * size * (primal + size),
            6 * faces * samples * size + 2 * faces * size * (primal + size),
        ),
        name="residuals",
    )(slot, scale, *canon, *beside, ordered, restore, handoff, mask)


def share_kernel(inflow, out):
    total = inflow[0]
    for q in range(1, inflow.shape[0]):
        total = total + inflow[q]
    out[...] = jnp.broadcast_to(total[None], out.shape)


def shared_sum(inflow, copies):
    members, share, channels = inflow.shape
    return pl.pallas_call(
        share_kernel,
        out_shape=jax.ShapeDtypeStruct((copies, share, channels), F32),
        compiler_params=params(8),
        cost_estimate=cost(members * share * channels, 4 * (copies + members) * share * channels),
        name="shared_sum",
    )(inflow)


def dual_kernel(first, slot, scale, masked, sort, mask, inverse, out):
    d = first + pl.program_id(0)
    faces, _, size = masked.shape
    total = None
    for g in range(faces):
        term = times(masked[g], inverse[g * size : (g + 1) * size, :])
        total = term if total is None else total + term
    high, low = split(total * (mask[slot[d]] * scale[d]))
    out[0] = times(high, sort[0]) + times(low, sort[0])


def dual(first, count, slot, scale, masked, sort, mask, inverse):
    faces, samples, size = masked.shape
    return pl.pallas_call(
        functools.partial(dual_kernel, first),
        out_shape=pltpu.HBM((count, samples, size), F32),
        grid_spec=pltpu.PrefetchScalarGridSpec(
            num_scalar_prefetch=1,
            grid=(count,),
            in_specs=[
                pl.BlockSpec(memory_space=pltpu.SMEM),
                resident(masked.shape),
                pl.BlockSpec((1, size, size), lambda i, slot: (first + i, 0, 0)),
                resident(mask.shape),
                pl.BlockSpec((faces * size, size), lambda i, slot: (0, slot[first + i])),
            ],
            out_specs=pl.BlockSpec((1, samples, size), lambda i, slot: (i, 0, 0)),
        ),
        compiler_params=params(16),
        cost_estimate=cost(
            2 * count * samples * size * (faces + 2) * size,
            2 * count * size * (faces + 1) * size + 6 * faces * samples * size,
        ),
        name=f"dual{first}",
    )(slot, scale, in_hbm(masked), in_hbm(sort), mask, in_hbm(inverse))


DOUBLING = (4, 2, 1)
DOUBLED_BITS = (0, 4, 2, 6, 1, 5, 3, 7)
TINY = 1e-30


def triple(value, high, low):
    value_high, value_low = split(value)
    return times(value_high, high) + (times(value_low, high) + times(value_high, low))


def maps_kernel(transfer, maps, product):
    group, channels, _ = transfer.shape
    own = lax.rem(lax.axis_index("sub"), group)
    total = None
    for k in range(group):
        bits = jnp.bitwise_xor(own, k)
        place = (bits & 1) * 4 + (bits & 2) + lax.shift_right_logical(bits, 2)
        value = transfer[place]
        high, low = split(value)
        maps[2 * k] = high
        maps[2 * k + 1] = low
        largest = jnp.max(jnp.abs(value), axis=1, keepdims=True)
        largest = jnp.maximum(jnp.max(largest, axis=0, keepdims=True), TINY)
        product[0, pl.ds(channels + k, 1), :] = jnp.broadcast_to(largest, (1, channels))
        scaled = value / largest
        total = scaled if total is None else triple(total, *split(scaled))
    product[0, pl.ds(0, channels), :] = total


def group_maps(transfer):
    group, channels, _ = transfer.shape
    return pl.pallas_call(
        maps_kernel,
        out_shape=[
            pltpu.HBM((2 * group, channels, channels), BF16),
            jax.ShapeDtypeStruct((1, channels + group, channels), F32),
        ],
        grid=(1,),
        in_specs=[resident(transfer.shape)],
        out_specs=[
            resident((2 * group, channels, channels)),
            resident((1, channels + group, channels)),
        ],
        compiler_params=params(8),
        cost_estimate=cost(6 * group * channels**3, 8 * group * channels * channels),
        name="group_maps",
    )(transfer)


def run_lines(state, inflow, maps, count):
    def step(k, value):
        return triple(value, maps[2 * k], maps[2 * k + 1]) + inflow[k]

    return lax.fori_loop(0, count, step, state)


def outflow_kernel(inflow, maps, out):
    lines, samples, channels = inflow.shape
    state = jnp.zeros((samples, channels), F32)
    for k in range(lines):
        state = triple(state, maps[2 * k], maps[2 * k + 1]) + inflow[k] if k else inflow[0]
    out[...] = state


def group_outflow(inflow, maps):
    lines, samples, channels = inflow.shape
    return pl.pallas_call(
        outflow_kernel,
        out_shape=jax.ShapeDtypeStruct((samples, channels), F32),
        grid=(1,),
        in_specs=[resident(inflow.shape), resident(maps.shape)],
        out_specs=IN_VMEM,
        compiler_params=params(8),
        cost_estimate=cost(
            6 * lines * samples * channels * channels, 4 * lines * channels * (samples + channels)
        ),
        name="group_outflow",
    )(inflow, in_hbm(maps))


def carried_kernel(products, inflow, maps, *refs):
    outflows, out = refs[:-1], refs[-1]
    lines, samples, channels = inflow.shape
    line = lax.axis_index("sub")
    group = lax.div(line, lines)
    state = jnp.zeros((samples, channels), F32)
    for step, outflow in zip(range(len(outflows), 0, -1), outflows):
        place = jnp.bitwise_xor(group, jnp.maximum(group - step, 0))
        value = triple(state, *split(products[place, pl.ds(0, channels), :]))
        for k in range(lines):
            value = value * products[place, pl.ds(channels + k, 1), :]
        state = jnp.where(group >= step, value + outflow[...], state)
    state = run_lines(state, inflow, maps, lax.rem(line, lines))
    out[...] = jnp.broadcast_to(state[None], out.shape)


def carried_states(outflows, products, inflow, maps, copies):
    lines, samples, channels = inflow.shape
    return pl.pallas_call(
        carried_kernel,
        out_shape=jax.ShapeDtypeStruct((copies, samples, channels), F32),
        grid=(1,),
        in_specs=[
            resident(products.shape),
            resident(inflow.shape),
            resident(maps.shape),
        ]
        + [resident((samples, channels))] * len(outflows),
        out_specs=IN_VMEM,
        compiler_params=params(8),
        cost_estimate=cost(
            6 * lines * samples * channels * channels, 8 * lines * channels * (samples + channels)
        ),
        name="carried_states",
    )(products, inflow, in_hbm(maps), *outflows)


def line_kernel(gathered, inverse, out):
    members, _, primal = gathered.shape
    member = lax.axis_index("coarse")
    total = None
    for i, bits in enumerate(GATHER_BITS):
        start = pl.multiple_of(jnp.bitwise_xor(member, bits) * primal, primal)
        term = times(gathered[i], inverse[pl.ds(start, primal), :])
        total = term if total is None else total + term
    out[...] = total


def line_base(gathered, inverse):
    members, samples, primal = gathered.shape
    return pl.pallas_call(
        line_kernel,
        out_shape=jax.ShapeDtypeStruct((samples, primal), F32),
        grid=(1,),
        in_specs=[resident(gathered.shape), resident(inverse.shape)],
        out_specs=IN_VMEM,
        compiler_params=params(12),
        cost_estimate=cost(
            2 * members * samples * primal * primal, 2 * members * primal * (samples + primal)
        ),
        name="line_base",
    )(gathered, in_hbm(inverse))


def extend_kernel(scale, base, carried, coupling, ordered_columns, dual0, dual1, *outs):
    high, low = split(carried[...])
    term = times(high, coupling[...]) + times(low, coupling[...])
    answer = (base[...] + term).astype(BF16)
    half = len(outs) // 2
    for d, out in enumerate(outs):
        value = dual0[d] if d < half else dual1[d - half]
        out[...] = (value + scale[d] * times(answer, ordered_columns[d])).astype(BF16)


def extend(scale, base, carried, coupling, ordered_columns, dual0, dual1):
    half, samples, size = dual0.shape
    faces = 2 * half
    primal = base.shape[1]
    return pl.pallas_call(
        extend_kernel,
        out_shape=[jax.ShapeDtypeStruct((samples, size), BF16)] * faces,
        grid=(1,),
        in_specs=[
            pl.BlockSpec(memory_space=pltpu.SMEM),
            IN_VMEM,
            IN_VMEM,
            resident(coupling.shape),
            resident(ordered_columns.shape),
            resident(dual0.shape),
            resident(dual1.shape),
        ],
        out_specs=[IN_VMEM] * faces,
        compiler_params=params(12),
        cost_estimate=cost(
            2 * faces * samples * size * primal, 6 * faces * samples * size + 2 * faces * size * primal
        ),
        name="extend",
    )(scale, base, carried, in_hbm(coupling), in_hbm(ordered_columns), in_hbm(dual0), in_hbm(dual1))


def finish_kernel(slot, *refs):
    d = pl.program_id(0)
    restore, out = refs[-2:]
    faces = (len(refs) - 2) // 2
    for i in range(faces):

        @pl.when(d == i)
        def _():
            value = sum_across(refs[i], refs[faces + i], i).astype(BF16)
            out[0] = times(value, restore[i]).astype(BF16)


def finish(slot, weighted, beside, restore):
    faces, size, _ = restore.shape
    samples = weighted[0].shape[0]
    return pl.pallas_call(
        finish_kernel,
        out_shape=jax.ShapeDtypeStruct((faces, samples, size), BF16),
        grid_spec=pltpu.PrefetchScalarGridSpec(
            num_scalar_prefetch=1,
            grid=(faces,),
            in_specs=[IN_VMEM] * (2 * faces + 1),
            out_specs=pl.BlockSpec((1, samples, size), lambda d, s: (s[d], 0, 0)),
        ),
        compiler_params=params(8),
        cost_estimate=cost(
            2 * faces * samples * size * size, 6 * faces * samples * size + 2 * faces * size * size
        ),
        name="finish",
    )(slot, *weighted, *beside, restore)


GROUP = 8
GATHER_STAGES = (2, 1, 4)
GATHER_BITS = (0, 2, 1, 3, 4, 6, 5, 7)


def exchange(value, axis, bit):
    return lax.ppermute(value, axis, [(i, i ^ bit) for i in range(lax.axis_size(axis))])


def doubled(value, axis, bit):
    return jnp.concatenate([value, exchange(value, axis, bit)])


def shifted(value, axis, step):
    count = lax.axis_size(axis)
    return lax.ppermute(value, axis, [(i, (i + step) % count) for i in range(count)])


def neighbours(faces):
    lower, upper, left, right = faces
    return (
        shifted(upper, "sub", 1),
        shifted(lower, "sub", -1),
        shifted(right, "coarse", 1),
        shifted(left, "coarse", -1),
    )


def per_device(
    residual_parts,
    face_slot,
    face_order,
    face_scale,
    vertex_unknowns,
    front_inverse,
    coarse_basis,
    coarse_inverse,
    thermal_handoff,
    chain_transfer,
    coupling_in,
):
    parts = residual_parts[0, 0]
    slot = face_slot[0, 0]
    order = face_order[0, 0]
    scale = face_scale[0, 0]
    faces, samples, size = parts.shape
    basis = coarse_basis[0, 0].reshape(faces, size, -1)
    lines, members = lax.axis_size("sub"), lax.axis_size("coarse")
    share = samples // members

    groups = lines // GROUP
    inside = [[a * GROUP + b for b in range(GROUP)] for a in range(groups)]
    copied = exchange(chain_transfer, "sub", DOUBLING[0])
    positions = lax.broadcasted_iota(jnp.int32, (vertex_unknowns.shape[2], faces * size), 1)
    hits = jnp.sum((vertex_unknowns[0, 0][:, None] == positions).astype(F32), axis=0)
    mask = (1.0 - hits).reshape(faces, 1, size)

    canon = to_canonical(slot, parts, order)
    beside = neighbours(canon)
    copied, basis, canon, mask = lax.optimization_barrier((copied, basis, canon, mask))
    transfer = jnp.concatenate([chain_transfer, copied])
    copied = exchange(transfer, "sub", DOUBLING[1])
    sort, restore, restore_near, ordered, ordered_columns = tables(slot, order, basis)
    masked, coarse_residual, heat = residuals(
        slot, scale, canon, beside, ordered, restore_near, thermal_handoff[0], mask
    )
    copied, heat = lax.optimization_barrier((copied, heat))
    transfer = doubled(jnp.concatenate([transfer, copied]), "sub", DOUBLING[2])

    channels = heat.shape[1]
    gathered = coarse_residual[None]
    received = exchange(gathered, "coarse", GATHER_STAGES[0])
    inflow = lax.all_to_all(heat.reshape(members, share, channels), "coarse", 0, 0)
    maps, product = group_maps(transfer)
    inflow, maps, product = lax.optimization_barrier((inflow, maps, product))
    inflow = shared_sum(inflow, GROUP)
    masked, received, inflow = lax.optimization_barrier((masked, received, inflow))

    inflow = lax.all_to_all(inflow, "sub", 0, 0, axis_index_groups=inside)
    others = exchange(product, "sub", GROUP)
    gathered = jnp.concatenate([gathered, received])
    received = exchange(gathered, "coarse", GATHER_STAGES[1])
    half = faces // 2
    dual0 = dual(0, half, slot, scale, masked, sort, mask, front_inverse[0, 0])
    inflow, others, dual0, masked = lax.optimization_barrier((inflow, others, dual0, masked))
    product = jnp.concatenate([product, others])
    others = exchange(product, "sub", 2 * GROUP)

    outflow = group_outflow(inflow, maps)
    masked, received, outflow = lax.optimization_barrier((masked, received, outflow))
    outflows = [shifted(outflow, "sub", GROUP * step) for step in range(groups - 1, 0, -1)]
    gathered = jnp.concatenate([gathered, received])
    masked, gathered = lax.optimization_barrier((masked, gathered))
    dual1 = dual(half, half, slot, scale, masked, sort, mask, front_inverse[0, 0])
    received = exchange(gathered, "coarse", GATHER_STAGES[2])
    outflows, others, dual1 = lax.optimization_barrier((outflows, others, dual1))
    product = jnp.concatenate([product, others])
    gathered = jnp.concatenate([gathered, received])
    carried = carried_states(outflows, product, inflow, maps, members)
    carried = lax.all_to_all(carried, "coarse", 0, 0).reshape(samples, channels)
    base = line_base(gathered, coarse_inverse[0])

    weighted = extend(scale, base, carried, coupling_in[0], ordered_columns, dual0, dual1)
    beside = neighbours(weighted)
    return finish(slot, weighted, beside, restore)[None, None]


def solution(mesh):
    placed = (
        P("sub", "coarse", None, None, None),
        P("sub", "coarse", None),
        P("sub", "coarse", None, None),
        P("sub", "coarse", None),
        P("sub", "coarse", None),
        P("sub", "coarse", None, None),
        P("sub", "coarse", None, None),
        P("sub", None, "coarse"),
        P("sub", None, None),
        P("sub", None, None),
        P("sub", None, "coarse"),
    )
    return jax.shard_map(
        per_device,
        mesh=mesh,
        in_specs=placed,
        out_specs=P("sub", "coarse", None, None, None),
        check_vma=False,
    )
```

```python
import functools

import jax
import jax.numpy as jnp
from jax import lax
from jax.experimental import pallas as pl
from jax.experimental.pallas import tpu as pltpu
from jax.sharding import PartitionSpec as P

BF16 = jnp.bfloat16
F32 = jnp.float32


def params(megabytes):
    return pltpu.CompilerParams(vmem_limit_bytes=megabytes << 20)


def cost(flops, bytes_accessed):
    return pl.CostEstimate(flops=flops, bytes_accessed=bytes_accessed, transcendentals=0)


def resident(shape):
    return pl.BlockSpec(shape, lambda *_: (0,) * len(shape))


IN_VMEM = pl.BlockSpec(memory_space=pltpu.VMEM)


def in_hbm(value):
    return pltpu.with_memory_space_constraint(value, pltpu.HBM)


def times(a, b):
    return jnp.dot(a, b, preferred_element_type=F32)


def times_columns(a, b):
    return lax.dot_general(a, b, (((0,), (0,)), ((), ())), preferred_element_type=F32)


def split(value):
    high = value.astype(BF16)
    return high, (value - high.astype(F32)).astype(BF16)


def sorting_table(order, face):
    size = order.shape[1]
    local = lax.broadcasted_iota(jnp.int32, (size, size), 0)
    return jnp.where(local == order[pl.ds(face, 1), :], 1.0, 0.0)


def canon_kernel(slot, parts, order, *outs):
    for d, out in enumerate(outs):
        s = slot[d]
        out[...] = times(parts[s], sorting_table(order, s).astype(BF16)).astype(BF16)


def to_canonical(slot, parts, order):
    faces, samples, size = parts.shape
    return pl.pallas_call(
        canon_kernel,
        out_shape=[jax.ShapeDtypeStruct((samples, size), BF16)] * faces,
        grid_spec=pltpu.PrefetchScalarGridSpec(
            num_scalar_prefetch=1,
            grid=(1,),
            in_specs=[resident(parts.shape), resident((faces, size))],
            out_specs=[IN_VMEM] * faces,
        ),
        compiler_params=params(8),
        cost_estimate=cost(2 * faces * samples * size * size, 4 * faces * samples * size),
        name="canon",
    )(slot, in_hbm(parts), in_hbm(order))


def tables_kernel(slot, order, basis, sort, restore, restore_near, ordered, ordered_columns):
    d = pl.program_id(0)
    table = sorting_table(order, slot[d])
    sort[0] = table.astype(BF16)
    restore[0] = table.T.astype(BF16)
    restore_near[0] = restore[0]
    ordered[0] = times(restore[0], basis[0]).astype(BF16)
    ordered_columns[0] = times_columns(basis[0], sort[0]).astype(BF16)


def tables(slot, order, basis):
    faces, size, primal = basis.shape

    def by_direction(*shape):
        return pl.BlockSpec((1,) + shape, lambda d, slot: (d, 0, 0))

    return pl.pallas_call(
        tables_kernel,
        out_shape=[
            pltpu.HBM((faces, size, size), BF16),
            pltpu.HBM((faces, size, size), BF16),
            jax.ShapeDtypeStruct((faces, size, size), BF16),
            jax.ShapeDtypeStruct((faces, size, primal), BF16),
            pltpu.HBM((faces, primal, size), BF16),
        ],
        grid_spec=pltpu.PrefetchScalarGridSpec(
            num_scalar_prefetch=1,
            grid=(faces,),
            in_specs=[
                resident((faces, size)),
                pl.BlockSpec((1, size, primal), lambda d, slot: (slot[d], 0, 0)),
            ],
            out_specs=[
                by_direction(size, size),
                by_direction(size, size),
                by_direction(size, size),
                by_direction(size, primal),
                by_direction(primal, size),
            ],
        ),
        compiler_params=params(12),
        cost_estimate=cost(
            4 * faces * size * size * primal, 4 * faces * size * size + 6 * faces * size * primal
        ),
        name="tables",
    )(slot, in_hbm(order), in_hbm(basis))


def has_neighbour(d):
    axis = "sub" if d < 2 else "coarse"
    place = lax.axis_index(axis)
    return place > 0 if d % 2 == 0 else place < lax.axis_size(axis) - 1


def sum_across(own, beside, d):
    own, beside = own[...].astype(F32), beside[...].astype(F32)
    return own + jnp.where(has_neighbour(d), beside, 0.0)


def residual_kernel(slot, scale, *refs):
    faces = scale.shape[0]
    canon, beside = refs[:faces], refs[faces : 2 * faces]
    ordered, restore, handoff, mask, masked, coarse, heat = refs[2 * faces :]
    total = None
    for d in range(faces):
        value = (scale[d] * sum_across(canon[d], beside[d], d)).astype(BF16)
        term = times(value, ordered[d])
        total = term if total is None else total + term
        s = slot[d]
        masked[s] = (times(value, restore[d]) * mask[s]).astype(BF16)
    rounded = total.astype(BF16)
    coarse[...] = rounded
    primal = rounded.shape[1]
    start = pl.multiple_of(lax.axis_index("coarse") * primal, primal)
    heat[...] = times(rounded, handoff[pl.ds(start, primal), :])


def residuals(slot, scale, canon, beside, ordered, restore, handoff, mask):
    faces, size, primal = ordered.shape
    samples = canon[0].shape[0]
    channels = handoff.shape[1]
    return pl.pallas_call(
        residual_kernel,
        out_shape=[
            pltpu.HBM((faces, samples, size), BF16),
            jax.ShapeDtypeStruct((samples, primal), BF16),
            jax.ShapeDtypeStruct((samples, channels), F32),
        ],
        grid_spec=pltpu.PrefetchScalarGridSpec(
            num_scalar_prefetch=1,
            grid=(1,),
            in_specs=[pl.BlockSpec(memory_space=pltpu.SMEM)] + [IN_VMEM] * (2 * faces + 4),
            out_specs=[resident((faces, samples, size)), IN_VMEM, IN_VMEM],
        ),
        compiler_params=params(8),
        cost_estimate=cost(
            2 * faces * samples * size * (primal + size),
            6 * faces * samples * size + 2 * faces * size * (primal + size),
        ),
        name="residuals",
    )(slot, scale, *canon, *beside, ordered, restore, handoff, mask)


def share_kernel(inflow, out):
    total = inflow[0]
    for q in range(1, inflow.shape[0]):
        total = total + inflow[q]
    out[...] = jnp.broadcast_to(total[None], out.shape)


def shared_sum(inflow, copies):
    members, share, channels = inflow.shape
    return pl.pallas_call(
        share_kernel,
        out_shape=jax.ShapeDtypeStruct((copies, share, channels), F32),
        compiler_params=params(8),
        cost_estimate=cost(members * share * channels, 4 * (copies + members) * share * channels),
        name="shared_sum",
    )(inflow)


def dual_kernel(first, slot, scale, masked, sort, mask, inverse, out):
    d = first + pl.program_id(0)
    faces, _, size = masked.shape
    total = None
    for g in range(faces):
        term = times(masked[g], inverse[g * size : (g + 1) * size, :])
        total = term if total is None else total + term
    high, low = split(total * (mask[slot[d]] * scale[d]))
    out[0] = times(high, sort[0]) + times(low, sort[0])


def dual(first, count, slot, scale, masked, sort, mask, inverse):
    faces, samples, size = masked.shape
    return pl.pallas_call(
        functools.partial(dual_kernel, first),
        out_shape=pltpu.HBM((count, samples, size), F32),
        grid_spec=pltpu.PrefetchScalarGridSpec(
            num_scalar_prefetch=1,
            grid=(count,),
            in_specs=[
                pl.BlockSpec(memory_space=pltpu.SMEM),
                resident(masked.shape),
                pl.BlockSpec((1, size, size), lambda i, slot: (first + i, 0, 0)),
                resident(mask.shape),
                pl.BlockSpec((faces * size, size), lambda i, slot: (0, slot[first + i])),
            ],
            out_specs=pl.BlockSpec((1, samples, size), lambda i, slot: (i, 0, 0)),
        ),
        compiler_params=params(16),
        cost_estimate=cost(
            2 * count * samples * size * (faces + 2) * size,
            2 * count * size * (faces + 1) * size + 6 * faces * samples * size,
        ),
        name=f"dual{first}",
    )(slot, scale, in_hbm(masked), in_hbm(sort), mask, in_hbm(inverse))


DOUBLING = (4, 2, 1)
DOUBLED_BITS = (0, 4, 2, 6, 1, 5, 3, 7)
TINY = 1e-30


def triple(value, high, low):
    value_high, value_low = split(value)
    return times(value_high, high) + (times(value_low, high) + times(value_high, low))


def maps_kernel(transfer, maps, product):
    group, channels, _ = transfer.shape
    own = lax.rem(lax.axis_index("sub"), group)
    total = None
    for k in range(group):
        bits = jnp.bitwise_xor(own, k)
        place = (bits & 1) * 4 + (bits & 2) + lax.shift_right_logical(bits, 2)
        value = transfer[place]
        high, low = split(value)
        maps[2 * k] = high
        maps[2 * k + 1] = low
        largest = jnp.max(jnp.abs(value), axis=1, keepdims=True)
        largest = jnp.maximum(jnp.max(largest, axis=0, keepdims=True), TINY)
        product[0, pl.ds(channels + k, 1), :] = jnp.broadcast_to(largest, (1, channels))
        scaled = value / largest
        total = scaled if total is None else triple(total, *split(scaled))
    product[0, pl.ds(0, channels), :] = total


def group_maps(transfer):
    group, channels, _ = transfer.shape
    return pl.pallas_call(
        maps_kernel,
        out_shape=[
            pltpu.HBM((2 * group, channels, channels), BF16),
            jax.ShapeDtypeStruct((1, channels + group, channels), F32),
        ],
        grid=(1,),
        in_specs=[resident(transfer.shape)],
        out_specs=[
            resident((2 * group, channels, channels)),
            resident((1, channels + group, channels)),
        ],
        compiler_params=params(8),
        cost_estimate=cost(6 * group * channels**3, 8 * group * channels * channels),
        name="group_maps",
    )(transfer)


def run_lines(state, inflow, maps, count):
    def step(k, value):
        return triple(value, maps[2 * k], maps[2 * k + 1]) + inflow[k]

    return lax.fori_loop(0, count, step, state)


def outflow_kernel(inflow, maps, out):
    lines, samples, channels = inflow.shape
    state = jnp.zeros((samples, channels), F32)
    for k in range(lines):
        state = triple(state, maps[2 * k], maps[2 * k + 1]) + inflow[k] if k else inflow[0]
    out[...] = state


def group_outflow(inflow, maps):
    lines, samples, channels = inflow.shape
    return pl.pallas_call(
        outflow_kernel,
        out_shape=jax.ShapeDtypeStruct((samples, channels), F32),
        grid=(1,),
        in_specs=[resident(inflow.shape), resident(maps.shape)],
        out_specs=IN_VMEM,
        compiler_params=params(8),
        cost_estimate=cost(
            6 * lines * samples * channels * channels, 4 * lines * channels * (samples + channels)
        ),
        name="group_outflow",
    )(inflow, in_hbm(maps))


def carried_kernel(products, inflow, maps, *refs):
    outflows, out = refs[:-1], refs[-1]
    lines, samples, channels = inflow.shape
    line = lax.axis_index("sub")
    group = lax.div(line, lines)
    state = jnp.zeros((samples, channels), F32)
    for step, outflow in zip(range(len(outflows), 0, -1), outflows):
        place = jnp.bitwise_xor(group, jnp.maximum(group - step, 0))
        value = triple(state, *split(products[place, pl.ds(0, channels), :]))
        for k in range(lines):
            value = value * products[place, pl.ds(channels + k, 1), :]
        state = jnp.where(group >= step, value + outflow[...], state)
    state = run_lines(state, inflow, maps, lax.rem(line, lines))
    out[...] = jnp.broadcast_to(state[None], out.shape)


def carried_states(outflows, products, inflow, maps, copies):
    lines, samples, channels = inflow.shape
    return pl.pallas_call(
        carried_kernel,
        out_shape=jax.ShapeDtypeStruct((copies, samples, channels), F32),
        grid=(1,),
        in_specs=[
            resident(products.shape),
            resident(inflow.shape),
            resident(maps.shape),
        ]
        + [resident((samples, channels))] * len(outflows),
        out_specs=IN_VMEM,
        compiler_params=params(8),
        cost_estimate=cost(
            6 * lines * samples * channels * channels, 8 * lines * channels * (samples + channels)
        ),
        name="carried_states",
    )(products, inflow, in_hbm(maps), *outflows)


def line_kernel(gathered, inverse, out):
    members, _, primal = gathered.shape
    member = lax.axis_index("coarse")
    total = None
    for i, bits in enumerate(GATHER_BITS):
        start = pl.multiple_of(jnp.bitwise_xor(member, bits) * primal, primal)
        term = times(gathered[i], inverse[pl.ds(start, primal), :])
        total = term if total is None else total + term
    out[...] = total


def line_base(gathered, inverse):
    members, samples, primal = gathered.shape
    return pl.pallas_call(
        line_kernel,
        out_shape=jax.ShapeDtypeStruct((samples, primal), F32),
        grid=(1,),
        in_specs=[resident(gathered.shape), resident(inverse.shape)],
        out_specs=IN_VMEM,
        compiler_params=params(12),
        cost_estimate=cost(
            2 * members * samples * primal * primal, 2 * members * primal * (samples + primal)
        ),
        name="line_base",
    )(gathered, in_hbm(inverse))


def extend_kernel(scale, base, carried, coupling, ordered_columns, dual0, dual1, *outs):
    high, low = split(carried[...])
    term = times(high, coupling[...]) + times(low, coupling[...])
    answer = (base[...] + term).astype(BF16)
    half = len(outs) // 2
    for d, out in enumerate(outs):
        value = dual0[d] if d < half else dual1[d - half]
        out[...] = (value + scale[d] * times(answer, ordered_columns[d])).astype(BF16)


def extend(scale, base, carried, coupling, ordered_columns, dual0, dual1):
    half, samples, size = dual0.shape
    faces = 2 * half
    primal = base.shape[1]
    return pl.pallas_call(
        extend_kernel,
        out_shape=[jax.ShapeDtypeStruct((samples, size), BF16)] * faces,
        grid=(1,),
        in_specs=[
            pl.BlockSpec(memory_space=pltpu.SMEM),
            IN_VMEM,
            IN_VMEM,
            resident(coupling.shape),
            resident(ordered_columns.shape),
            resident(dual0.shape),
            resident(dual1.shape),
        ],
        out_specs=[IN_VMEM] * faces,
        compiler_params=params(12),
        cost_estimate=cost(
            2 * faces * samples * size * primal, 6 * faces * samples * size + 2 * faces * size * primal
        ),
        name="extend",
    )(scale, base, carried, in_hbm(coupling), in_hbm(ordered_columns), in_hbm(dual0), in_hbm(dual1))


def finish_kernel(slot, *refs):
    d = pl.program_id(0)
    restore, out = refs[-2:]
    faces = (len(refs) - 2) // 2
    for i in range(faces):

        @pl.when(d == i)
        def _():
            value = sum_across(refs[i], refs[faces + i], i).astype(BF16)
            out[0] = times(value, restore[i]).astype(BF16)


def finish(slot, weighted, beside, restore):
    faces, size, _ = restore.shape
    samples = weighted[0].shape[0]
    return pl.pallas_call(
        finish_kernel,
        out_shape=jax.ShapeDtypeStruct((faces, samples, size), BF16),
        grid_spec=pltpu.PrefetchScalarGridSpec(
            num_scalar_prefetch=1,
            grid=(faces,),
            in_specs=[IN_VMEM] * (2 * faces + 1),
            out_specs=pl.BlockSpec((1, samples, size), lambda d, s: (s[d], 0, 0)),
        ),
        compiler_params=params(8),
        cost_estimate=cost(
            2 * faces * samples * size * size, 6 * faces * samples * size + 2 * faces * size * size
        ),
        name="finish",
    )(slot, *weighted, *beside, restore)


GROUP = 8
GATHER_STAGES = (2, 1, 4)
GATHER_BITS = (0, 2, 1, 3, 4, 6, 5, 7)


def exchange(value, axis, bit):
    return lax.ppermute(value, axis, [(i, i ^ bit) for i in range(lax.axis_size(axis))])


def doubled(value, axis, bit):
    return jnp.concatenate([value, exchange(value, axis, bit)])


def shifted(value, axis, step):
    count = lax.axis_size(axis)
    return lax.ppermute(value, axis, [(i, (i + step) % count) for i in range(count)])


def neighbours(faces):
    lower, upper, left, right = faces
    return (
        shifted(upper, "sub", 1),
        shifted(lower, "sub", -1),
        shifted(right, "coarse", 1),
        shifted(left, "coarse", -1),
    )


def per_device(
    residual_parts,
    face_slot,
    face_order,
    face_scale,
    vertex_unknowns,
    front_inverse,
    coarse_basis,
    coarse_inverse,
    thermal_handoff,
    chain_transfer,
    coupling_in,
):
    parts = residual_parts[0, 0]
    slot = face_slot[0, 0]
    order = face_order[0, 0]
    scale = face_scale[0, 0]
    faces, samples, size = parts.shape
    basis = coarse_basis[0, 0].reshape(faces, size, -1)
    lines, members = lax.axis_size("sub"), lax.axis_size("coarse")
    share = samples // members

    groups = lines // GROUP
    inside = [[a * GROUP + b for b in range(GROUP)] for a in range(groups)]
    copied = exchange(chain_transfer, "sub", DOUBLING[0])
    positions = lax.broadcasted_iota(jnp.int32, (vertex_unknowns.shape[2], faces * size), 1)
    hits = jnp.sum((vertex_unknowns[0, 0][:, None] == positions).astype(F32), axis=0)
    mask = (1.0 - hits).reshape(faces, 1, size)

    canon = to_canonical(slot, parts, order)
    beside = neighbours(canon)
    copied, basis, canon, mask = lax.optimization_barrier((copied, basis, canon, mask))
    transfer = jnp.concatenate([chain_transfer, copied])
    copied = exchange(transfer, "sub", DOUBLING[1])
    sort, restore, restore_near, ordered, ordered_columns = tables(slot, order, basis)
    masked, coarse_residual, heat = residuals(
        slot, scale, canon, beside, ordered, restore_near, thermal_handoff[0], mask
    )
    copied, heat = lax.optimization_barrier((copied, heat))
    transfer = doubled(jnp.concatenate([transfer, copied]), "sub", DOUBLING[2])

    channels = heat.shape[1]
    gathered = coarse_residual[None]
    received = exchange(gathered, "coarse", GATHER_STAGES[0])
    inflow = lax.all_to_all(heat.reshape(members, share, channels), "coarse", 0, 0)
    maps, product = group_maps(transfer)
    inflow, maps, product = lax.optimization_barrier((inflow, maps, product))
    inflow = shared_sum(inflow, GROUP)
    masked, inflow = lax.optimization_barrier((masked, inflow))

    inflow = lax.all_to_all(inflow, "sub", 0, 0, axis_index_groups=inside)
    others = exchange(product, "sub", GROUP)
    gathered = jnp.concatenate([gathered, received])
    received = exchange(gathered, "coarse", GATHER_STAGES[1])
    half = faces // 2
    dual0 = dual(0, half, slot, scale, masked, sort, mask, front_inverse[0, 0])
    inflow, others, dual0, masked = lax.optimization_barrier((inflow, others, dual0, masked))
    product = jnp.concatenate([product, others])
    others = exchange(product, "sub", 2 * GROUP)

    outflow = group_outflow(inflow, maps)
    masked, received, outflow = lax.optimization_barrier((masked, received, outflow))
    outflows = [shifted(outflow, "sub", GROUP * step) for step in range(groups - 1, 0, -1)]
    gathered = jnp.concatenate([gathered, received])
    masked, gathered = lax.optimization_barrier((masked, gathered))
    dual1 = dual(half, half, slot, scale, masked, sort, mask, front_inverse[0, 0])
    received = exchange(gathered, "coarse", GATHER_STAGES[2])
    outflows, others, dual1 = lax.optimization_barrier((outflows, others, dual1))
    product = jnp.concatenate([product, others])
    gathered = jnp.concatenate([gathered, received])
    carried = carried_states(outflows, product, inflow, maps, members)
    carried = lax.all_to_all(carried, "coarse", 0, 0).reshape(samples, channels)
    base = line_base(gathered, coarse_inverse[0])

    weighted = extend(scale, base, carried, coupling_in[0], ordered_columns, dual0, dual1)
    beside = neighbours(weighted)
    return finish(slot, weighted, beside, restore)[None, None]


def solution(mesh):
    placed = (
        P("sub", "coarse", None, None, None),
        P("sub", "coarse", None),
        P("sub", "coarse", None, None),
        P("sub", "coarse", None),
        P("sub", "coarse", None),
        P("sub", "coarse", None, None),
        P("sub", "coarse", None, None),
        P("sub", None, "coarse"),
        P("sub", None, None),
        P("sub", None, None),
        P("sub", None, "coarse"),
    )
    return jax.shard_map(
        per_device,
        mesh=mesh,
        in_specs=placed,
        out_specs=P("sub", "coarse", None, None, None),
        check_vma=False,
    )
```

```python
import functools

import jax
import jax.numpy as jnp
from jax import lax
from jax.experimental import pallas as pl
from jax.experimental.pallas import tpu as pltpu
from jax.sharding import PartitionSpec as P

BF16 = jnp.bfloat16
F32 = jnp.float32


def params(megabytes):
    return pltpu.CompilerParams(vmem_limit_bytes=megabytes << 20)


def cost(flops, bytes_accessed):
    return pl.CostEstimate(flops=flops, bytes_accessed=bytes_accessed, transcendentals=0)


def resident(shape):
    return pl.BlockSpec(shape, lambda *_: (0,) * len(shape))


IN_VMEM = pl.BlockSpec(memory_space=pltpu.VMEM)


def in_hbm(value):
    return pltpu.with_memory_space_constraint(value, pltpu.HBM)


def times(a, b):
    return jnp.dot(a, b, preferred_element_type=F32)


def times_columns(a, b):
    return lax.dot_general(a, b, (((0,), (0,)), ((), ())), preferred_element_type=F32)


def split(value):
    high = value.astype(BF16)
    return high, (value - high.astype(F32)).astype(BF16)


def sorting_table(order, face):
    size = order.shape[1]
    local = lax.broadcasted_iota(jnp.int32, (size, size), 0)
    return jnp.where(local == order[pl.ds(face, 1), :], 1.0, 0.0)


def canon_kernel(slot, parts, order, *outs):
    for d, out in enumerate(outs):
        s = slot[d]
        out[...] = times(parts[s], sorting_table(order, s).astype(BF16)).astype(BF16)


def to_canonical(slot, parts, order):
    faces, samples, size = parts.shape
    return pl.pallas_call(
        canon_kernel,
        out_shape=[jax.ShapeDtypeStruct((samples, size), BF16)] * faces,
        grid_spec=pltpu.PrefetchScalarGridSpec(
            num_scalar_prefetch=1,
            grid=(1,),
            in_specs=[resident(parts.shape), resident((faces, size))],
            out_specs=[IN_VMEM] * faces,
        ),
        compiler_params=params(8),
        cost_estimate=cost(2 * faces * samples * size * size, 4 * faces * samples * size),
        name="canon",
    )(in_hbm(slot), in_hbm(parts), in_hbm(order))


def tables_kernel(slot, order, basis, sort, restore, restore_near, ordered, ordered_columns):
    d = pl.program_id(0)
    table = sorting_table(order, slot[d])
    sort[0] = table.astype(BF16)
    restore[0] = table.T.astype(BF16)
    restore_near[0] = restore[0]
    ordered[0] = times(restore[0], basis[0]).astype(BF16)
    ordered_columns[0] = times_columns(basis[0], sort[0]).astype(BF16)


def tables(slot, order, basis):
    faces, size, primal = basis.shape

    def by_direction(*shape):
        return pl.BlockSpec((1,) + shape, lambda d, slot: (d, 0, 0))

    return pl.pallas_call(
        tables_kernel,
        out_shape=[
            pltpu.HBM((faces, size, size), BF16),
            pltpu.HBM((faces, size, size), BF16),
            jax.ShapeDtypeStruct((faces, size, size), BF16),
            jax.ShapeDtypeStruct((faces, size, primal), BF16),
            pltpu.HBM((faces, primal, size), BF16),
        ],
        grid_spec=pltpu.PrefetchScalarGridSpec(
            num_scalar_prefetch=1,
            grid=(faces,),
            in_specs=[
                resident((faces, size)),
                pl.BlockSpec((1, size, primal), lambda d, slot: (slot[d], 0, 0)),
            ],
            out_specs=[
                by_direction(size, size),
                by_direction(size, size),
                by_direction(size, size),
                by_direction(size, primal),
                by_direction(primal, size),
            ],
        ),
        compiler_params=params(12),
        cost_estimate=cost(
            4 * faces * size * size * primal, 4 * faces * size * size + 6 * faces * size * primal
        ),
        name="tables",
    )(slot, in_hbm(order), in_hbm(basis))


def has_neighbour(d):
    axis = "sub" if d < 2 else "coarse"
    place = lax.axis_index(axis)
    return place > 0 if d % 2 == 0 else place < lax.axis_size(axis) - 1


def sum_across(own, beside, d):
    own, beside = own[...].astype(F32), beside[...].astype(F32)
    return own + jnp.where(has_neighbour(d), beside, 0.0)


def residual_kernel(slot, scale, *refs):
    faces = scale.shape[0]
    canon, beside = refs[:faces], refs[faces : 2 * faces]
    ordered, restore, handoff, mask, masked, coarse, heat = refs[2 * faces :]
    total = None
    for d in range(faces):
        value = (scale[d] * sum_across(canon[d], beside[d], d)).astype(BF16)
        term = times(value, ordered[d])
        total = term if total is None else total + term
        s = slot[d]
        masked[s] = (times(value, restore[d]) * mask[s]).astype(BF16)
    rounded = total.astype(BF16)
    coarse[...] = rounded
    primal = rounded.shape[1]
    start = pl.multiple_of(lax.axis_index("coarse") * primal, primal)
    heat[...] = times(rounded, handoff[pl.ds(start, primal), :])


def residuals(slot, scale, canon, beside, ordered, restore, handoff, mask):
    faces, size, primal = ordered.shape
    samples = canon[0].shape[0]
    channels = handoff.shape[1]
    return pl.pallas_call(
        residual_kernel,
        out_shape=[
            pltpu.HBM((faces, samples, size), BF16),
            jax.ShapeDtypeStruct((samples, primal), BF16),
            jax.ShapeDtypeStruct((samples, channels), F32),
        ],
        grid_spec=pltpu.PrefetchScalarGridSpec(
            num_scalar_prefetch=1,
            grid=(1,),
            in_specs=[pl.BlockSpec(memory_space=pltpu.SMEM)] + [IN_VMEM] * (2 * faces + 4),
            out_specs=[resident((faces, samples, size)), IN_VMEM, IN_VMEM],
        ),
        compiler_params=params(8),
        cost_estimate=cost(
            2 * faces * samples * size * (primal + size),
            6 * faces * samples * size + 2 * faces * size * (primal + size),
        ),
        name="residuals",
    )(slot, scale, *canon, *beside, ordered, restore, handoff, mask)


def share_kernel(inflow, out):
    total = inflow[0]
    for q in range(1, inflow.shape[0]):
        total = total + inflow[q]
    out[...] = jnp.broadcast_to(total[None], out.shape)


def shared_sum(inflow, copies):
    members, share, channels = inflow.shape
    return pl.pallas_call(
        share_kernel,
        out_shape=jax.ShapeDtypeStruct((copies, share, channels), F32),
        compiler_params=params(8),
        cost_estimate=cost(members * share * channels, 4 * (copies + members) * share * channels),
        name="shared_sum",
    )(inflow)


def dual_kernel(first, slot, scale, masked, sort, mask, inverse, out):
    d = first + pl.program_id(0)
    faces, _, size = masked.shape
    total = None
    for g in range(faces):
        term = times(masked[g], inverse[g * size : (g + 1) * size, :])
        total = term if total is None else total + term
    high, low = split(total * (mask[slot[d]] * scale[d]))
    out[0] = times(high, sort[0]) + times(low, sort[0])


def dual(first, count, slot, scale, masked, sort, mask, inverse):
    faces, samples, size = masked.shape
    return pl.pallas_call(
        functools.partial(dual_kernel, first),
        out_shape=pltpu.HBM((count, samples, size), F32),
        grid_spec=pltpu.PrefetchScalarGridSpec(
            num_scalar_prefetch=1,
            grid=(count,),
            in_specs=[
                pl.BlockSpec(memory_space=pltpu.SMEM),
                resident(masked.shape),
                pl.BlockSpec((1, size, size), lambda i, slot: (first + i, 0, 0)),
                resident(mask.shape),
                pl.BlockSpec((faces * size, size), lambda i, slot: (0, slot[first + i])),
            ],
            out_specs=pl.BlockSpec((1, samples, size), lambda i, slot: (i, 0, 0)),
        ),
        compiler_params=params(16),
        cost_estimate=cost(
            2 * count * samples * size * (faces + 2) * size,
            2 * count * size * (faces + 1) * size + 6 * faces * samples * size,
        ),
        name=f"dual{first}",
    )(slot, scale, in_hbm(masked), in_hbm(sort), mask, in_hbm(inverse))


DOUBLING = (4, 2, 1)
DOUBLED_BITS = (0, 4, 2, 6, 1, 5, 3, 7)
TINY = 1e-30


def triple(value, high, low):
    value_high, value_low = split(value)
    return times(value_high, high) + (times(value_low, high) + times(value_high, low))


def maps_kernel(transfer, maps, product):
    group, channels, _ = transfer.shape
    own = lax.rem(lax.axis_index("sub"), group)
    total = None
    for k in range(group):
        bits = jnp.bitwise_xor(own, k)
        place = (bits & 1) * 4 + (bits & 2) + lax.shift_right_logical(bits, 2)
        value = transfer[place]
        high, low = split(value)
        maps[2 * k] = high
        maps[2 * k + 1] = low
        largest = jnp.max(jnp.abs(value), axis=1, keepdims=True)
        largest = jnp.maximum(jnp.max(largest, axis=0, keepdims=True), TINY)
        product[0, pl.ds(channels + k, 1), :] = jnp.broadcast_to(largest, (1, channels))
        scaled = value / largest
        total = scaled if total is None else triple(total, *split(scaled))
    product[0, pl.ds(0, channels), :] = total


def group_maps(transfer):
    group, channels, _ = transfer.shape
    return pl.pallas_call(
        maps_kernel,
        out_shape=[
            pltpu.HBM((2 * group, channels, channels), BF16),
            jax.ShapeDtypeStruct((1, channels + group, channels), F32),
        ],
        grid=(1,),
        in_specs=[resident(transfer.shape)],
        out_specs=[
            resident((2 * group, channels, channels)),
            resident((1, channels + group, channels)),
        ],
        compiler_params=params(8),
        cost_estimate=cost(6 * group * channels**3, 8 * group * channels * channels),
        name="group_maps",
    )(transfer)


def run_lines(state, inflow, maps, count):
    def step(k, value):
        return triple(value, maps[2 * k], maps[2 * k + 1]) + inflow[k]

    return lax.fori_loop(0, count, step, state)


def outflow_kernel(inflow, maps, out):
    lines, samples, channels = inflow.shape
    state = jnp.zeros((samples, channels), F32)
    for k in range(lines):
        state = triple(state, maps[2 * k], maps[2 * k + 1]) + inflow[k] if k else inflow[0]
    out[...] = state


def group_outflow(inflow, maps):
    lines, samples, channels = inflow.shape
    return pl.pallas_call(
        outflow_kernel,
        out_shape=jax.ShapeDtypeStruct((samples, channels), F32),
        grid=(1,),
        in_specs=[resident(inflow.shape), resident(maps.shape)],
        out_specs=IN_VMEM,
        compiler_params=params(8),
        cost_estimate=cost(
            6 * lines * samples * channels * channels, 4 * lines * channels * (samples + channels)
        ),
        name="group_outflow",
    )(inflow, in_hbm(maps))


def carried_kernel(products, inflow, maps, *refs):
    outflows, out = refs[:-1], refs[-1]
    lines, samples, channels = inflow.shape
    line = lax.axis_index("sub")
    group = lax.div(line, lines)
    state = jnp.zeros((samples, channels), F32)
    for step, outflow in zip(range(len(outflows), 0, -1), outflows):
        place = jnp.bitwise_xor(group, jnp.maximum(group - step, 0))
        value = triple(state, *split(products[place, pl.ds(0, channels), :]))
        for k in range(lines):
            value = value * products[place, pl.ds(channels + k, 1), :]
        state = jnp.where(group >= step, value + outflow[...], state)
    state = run_lines(state, inflow, maps, lax.rem(line, lines))
    out[...] = jnp.broadcast_to(state[None], out.shape)


def carried_states(outflows, products, inflow, maps, copies):
    lines, samples, channels = inflow.shape
    return pl.pallas_call(
        carried_kernel,
        out_shape=jax.ShapeDtypeStruct((copies, samples, channels), F32),
        grid=(1,),
        in_specs=[
            resident(products.shape),
            resident(inflow.shape),
            resident(maps.shape),
        ]
        + [resident((samples, channels))] * len(outflows),
        out_specs=IN_VMEM,
        compiler_params=params(8),
        cost_estimate=cost(
            6 * lines * samples * channels * channels, 8 * lines * channels * (samples + channels)
        ),
        name="carried_states",
    )(products, inflow, in_hbm(maps), *outflows)


def line_kernel(gathered, inverse, out):
    members, _, primal = gathered.shape
    member = lax.axis_index("coarse")
    total = None
    for i, bits in enumerate(GATHER_BITS):
        start = pl.multiple_of(jnp.bitwise_xor(member, bits) * primal, primal)
        term = times(gathered[i], inverse[pl.ds(start, primal), :])
        total = term if total is None else total + term
    out[...] = total


def line_base(gathered, inverse):
    members, samples, primal = gathered.shape
    return pl.pallas_call(
        line_kernel,
        out_shape=jax.ShapeDtypeStruct((samples, primal), F32),
        grid=(1,),
        in_specs=[resident(gathered.shape), resident(inverse.shape)],
        out_specs=IN_VMEM,
        compiler_params=params(12),
        cost_estimate=cost(
            2 * members * samples * primal * primal, 2 * members * primal * (samples + primal)
        ),
        name="line_base",
    )(gathered, in_hbm(inverse))


def extend_kernel(scale, base, carried, coupling, ordered_columns, dual0, dual1, *outs):
    high, low = split(carried[...])
    term = times(high, coupling[...]) + times(low, coupling[...])
    answer = (base[...] + term).astype(BF16)
    half = len(outs) // 2
    for d, out in enumerate(outs):
        value = dual0[d] if d < half else dual1[d - half]
        out[...] = (value + scale[d] * times(answer, ordered_columns[d])).astype(BF16)


def extend(scale, base, carried, coupling, ordered_columns, dual0, dual1):
    half, samples, size = dual0.shape
    faces = 2 * half
    primal = base.shape[1]
    return pl.pallas_call(
        extend_kernel,
        out_shape=[jax.ShapeDtypeStruct((samples, size), BF16)] * faces,
        grid=(1,),
        in_specs=[
            pl.BlockSpec(memory_space=pltpu.SMEM),
            IN_VMEM,
            IN_VMEM,
            resident(coupling.shape),
            resident(ordered_columns.shape),
            resident(dual0.shape),
            resident(dual1.shape),
        ],
        out_specs=[IN_VMEM] * faces,
        compiler_params=params(12),
        cost_estimate=cost(
            2 * faces * samples * size * primal, 6 * faces * samples * size + 2 * faces * size * primal
        ),
        name="extend",
    )(scale, base, carried, in_hbm(coupling), in_hbm(ordered_columns), in_hbm(dual0), in_hbm(dual1))


def finish_kernel(slot, *refs):
    d = pl.program_id(0)
    restore, out = refs[-2:]
    faces = (len(refs) - 2) // 2
    for i in range(faces):

        @pl.when(d == i)
        def _():
            value = sum_across(refs[i], refs[faces + i], i).astype(BF16)
            out[0] = times(value, restore[i]).astype(BF16)


def finish(slot, weighted, beside, restore):
    faces, size, _ = restore.shape
    samples = weighted[0].shape[0]
    return pl.pallas_call(
        finish_kernel,
        out_shape=jax.ShapeDtypeStruct((faces, samples, size), BF16),
        grid_spec=pltpu.PrefetchScalarGridSpec(
            num_scalar_prefetch=1,
            grid=(faces,),
            in_specs=[IN_VMEM] * (2 * faces + 1),
            out_specs=pl.BlockSpec((1, samples, size), lambda d, s: (s[d], 0, 0)),
        ),
        compiler_params=params(8),
        cost_estimate=cost(
            2 * faces * samples * size * size, 6 * faces * samples * size + 2 * faces * size * size
        ),
        name="finish",
    )(slot, *weighted, *beside, restore)


GROUP = 8
GATHER_STAGES = (2, 1, 4)
GATHER_BITS = (0, 2, 1, 3, 4, 6, 5, 7)


def exchange(value, axis, bit):
    return lax.ppermute(value, axis, [(i, i ^ bit) for i in range(lax.axis_size(axis))])


def doubled(value, axis, bit):
    return jnp.concatenate([value, exchange(value, axis, bit)])


def shifted(value, axis, step):
    count = lax.axis_size(axis)
    return lax.ppermute(value, axis, [(i, (i + step) % count) for i in range(count)])


def neighbours(faces):
    lower, upper, left, right = faces
    return (
        shifted(upper, "sub", 1),
        shifted(lower, "sub", -1),
        shifted(right, "coarse", 1),
        shifted(left, "coarse", -1),
    )


def per_device(
    residual_parts,
    face_slot,
    face_order,
    face_scale,
    vertex_unknowns,
    front_inverse,
    coarse_basis,
    coarse_inverse,
    thermal_handoff,
    chain_transfer,
    coupling_in,
):
    parts = residual_parts[0, 0]
    slot = face_slot[0, 0]
    order = face_order[0, 0]
    scale = face_scale[0, 0]
    faces, samples, size = parts.shape
    basis = coarse_basis[0, 0].reshape(faces, size, -1)
    lines, members = lax.axis_size("sub"), lax.axis_size("coarse")
    share = samples // members

    groups = lines // GROUP
    inside = [[a * GROUP + b for b in range(GROUP)] for a in range(groups)]
    copied = exchange(chain_transfer, "sub", DOUBLING[0])
    positions = lax.broadcasted_iota(jnp.int32, (vertex_unknowns.shape[2], faces * size), 1)
    hits = jnp.sum((vertex_unknowns[0, 0][:, None] == positions).astype(F32), axis=0)
    mask = (1.0 - hits).reshape(faces, 1, size)

    canon = to_canonical(slot, parts, order)
    beside = neighbours(canon)
    copied, basis, canon, mask = lax.optimization_barrier((copied, basis, canon, mask))
    transfer = jnp.concatenate([chain_transfer, copied])
    copied = exchange(transfer, "sub", DOUBLING[1])
    sort, restore, restore_near, ordered, ordered_columns = tables(slot, order, basis)
    masked, coarse_residual, heat = residuals(
        slot, scale, canon, beside, ordered, restore_near, thermal_handoff[0], mask
    )
    copied, heat = lax.optimization_barrier((copied, heat))
    transfer = doubled(jnp.concatenate([transfer, copied]), "sub", DOUBLING[2])

    channels = heat.shape[1]
    gathered = coarse_residual[None]
    received = exchange(gathered, "coarse", GATHER_STAGES[0])
    inflow = lax.all_to_all(heat.reshape(members, share, channels), "coarse", 0, 0)
    maps, product = group_maps(transfer)
    inflow, maps, product = lax.optimization_barrier((inflow, maps, product))
    inflow = shared_sum(inflow, GROUP)
    masked, inflow = lax.optimization_barrier((masked, inflow))

    inflow = lax.all_to_all(inflow, "sub", 0, 0, axis_index_groups=inside)
    others = exchange(product, "sub", GROUP)
    gathered = jnp.concatenate([gathered, received])
    received = exchange(gathered, "coarse", GATHER_STAGES[1])
    half = faces // 2
    dual0 = dual(0, half, slot, scale, masked, sort, mask, front_inverse[0, 0])
    inflow, others, dual0, masked = lax.optimization_barrier((inflow, others, dual0, masked))
    product = jnp.concatenate([product, others])
    others = exchange(product, "sub", 2 * GROUP)

    outflow = group_outflow(inflow, maps)
    masked, received, outflow = lax.optimization_barrier((masked, received, outflow))
    outflows = [shifted(outflow, "sub", GROUP * step) for step in range(groups - 1, 0, -1)]
    gathered = jnp.concatenate([gathered, received])
    masked, gathered = lax.optimization_barrier((masked, gathered))
    dual1 = dual(half, half, slot, scale, masked, sort, mask, front_inverse[0, 0])
    received = exchange(gathered, "coarse", GATHER_STAGES[2])
    outflows, others, dual1 = lax.optimization_barrier((outflows, others, dual1))
    product = jnp.concatenate([product, others])
    gathered = jnp.concatenate([gathered, received])
    carried = carried_states(outflows, product, inflow, maps, members)
    carried = lax.all_to_all(carried, "coarse", 0, 0).reshape(samples, channels)
    base = line_base(gathered, coarse_inverse[0])

    weighted = extend(scale, base, carried, coupling_in[0], ordered_columns, dual0, dual1)
    beside = neighbours(weighted)
    return finish(slot, weighted, beside, restore)[None, None]


def solution(mesh):
    placed = (
        P("sub", "coarse", None, None, None),
        P("sub", "coarse", None),
        P("sub", "coarse", None, None),
        P("sub", "coarse", None),
        P("sub", "coarse", None),
        P("sub", "coarse", None, None),
        P("sub", "coarse", None, None),
        P("sub", None, "coarse"),
        P("sub", None, None),
        P("sub", None, None),
        P("sub", None, "coarse"),
    )
    return jax.shard_map(
        per_device,
        mesh=mesh,
        in_specs=placed,
        out_specs=P("sub", "coarse", None, None, None),
        check_vma=False,
    )
```
